32 devices in a mesh: groups: 2 (over y), ctx: 16 (over z, x, core).
Axes of the slice: x: 2, y: 2, z: 4, core: 2. Of those that a mesh axis runs over, the one named last changes fastest.
Arguments:
- hidden: bfloat16 [4, 4, 8192], P(None, 'groups', 'ctx'), parts along dimension 1, may hold values from -6 to 6
- norm_gain: bfloat16 [8192], P('ctx'), may hold values from 0.5 to 1.5
- w_query: bfloat16 [8192, 8192], P('ctx')
- w_key: bfloat16 [8192, 1024], P('ctx'), may hold values from -0.25 to 0.25
- w_value: bfloat16 [8192, 1024], P('ctx'), may hold values from -0.125 to 0.125
- w_output: bfloat16 [8192, 8192], P('ctx'), may hold values from -0.09375 to 0.09375
- key_cache: bfloat16 [512, 128, 8, 128], P(('groups', 'ctx')), parts along dimension 0, may hold values from -6 to 6
- value_cache: bfloat16 [512, 128, 8, 128], P(('groups', 'ctx')), parts along dimension 0, may hold values from -6 to 6
- retrieval: int32 [8], replicated, may hold values from 0 to 1, as said below
- page_table: int32 [4, 128], P('groups'), parts along dimension 0, may hold values from 0 to 255, as said below
- lengths: int32 [4], P('groups'), parts along dimension 0, may hold values from 4096 to 16384, as said below
- window_start: int32 [4], P('groups'), parts along dimension 0, may hold values from 2945 to 15360, as said below
Outputs:
- attention_out: bfloat16 [4, 4, 8192], P(None, 'groups', 'ctx'), parts along dimension 1
The draws below stay inside these ranges and needn't reach their ends.
There are 2 independent parts, one for each index of `groups`. The reference program is written for one: setup_inputs(seed, part) draws one part's arguments, and reference() takes and returns one part's arrays. A program takes and returns all parts, laid end to end along the dimension named above; an argument that names none is the same for every part. Nothing has to cross between parts.
Inputs may be any that keep to these rules, and one draw needn't show every extreme that they name: `retrieval`: at least one key/value head of each kind. `page_table`: every page number appears exactly once; page g is row g of key_cache and value_cache. `lengths`: some request has exactly 16384 cached positions. lengths[b] - 1152 < window_start[b] <= lengths[b] - 1024.
All inputs are finite; a program needn't handle non-finite values.
Results may differ from the reference program's by a relative error of at most 0.0034.
The reference program's roundings to bfloat16 on the way (of `normed`, `query` and `attended`) count: a program that leaves them out, or rounds other values in their place, can miss the bound.
Values sent between devices are 32-bit elements; how exact they have to be, the bound alone decides.
A program may use at most 128 MiB of HBM per device.

```python
import math
import jax
import jax.numpy as jnp
from jax import lax

D = 8192
HEADS = 64
KV_HEADS = 8
HEAD_DIM = 128
STEPS = 4
BATCH = 2
PAGE = 128
WINDOW = 1024
SINKS = 4
PAGES_DEV = 16
BLOCKS = 128
CAP = 16384
N_CTX = 16


def request_bounds(key):
    base_key = jax.random.fold_in(key, 11)
    key_len, key_full, key_back = jax.random.split(base_key, 3)
    lowest = max(CAP // 4, WINDOW + 2 * PAGE)
    drawn = jax.random.randint(key_len, (BATCH,), lowest, CAP + 1)
    full_req = jax.random.randint(key_full, (), 0, BATCH)
    is_full = jnp.arange(BATCH) == full_req
    drawn = jnp.where(is_full, CAP, drawn)
    back_off = jax.random.randint(key_back, (BATCH,), 0, PAGE)
    back_off = jnp.where(is_full, 0, back_off)
    starts = drawn - WINDOW - back_off
    return (drawn.astype(jnp.int32), starts.astype(jnp.int32))


def draw_lengths(key, part):
    return request_bounds(key)[0]


def draw_window_start(key, part):
    return request_bounds(key)[1]


def draw_page_table(key, part):
    order = jax.random.permutation(jax.random.fold_in(key, 3), BATCH * BLOCKS)
    return order.reshape(BATCH, BLOCKS).astype(jnp.int32)


def draw_retrieval(key, part):
    key_count, key_perm = jax.random.split(jax.random.fold_in(key, 5), 2)
    count_full = jax.random.randint(key_count, (), 1, KV_HEADS)
    ranking = jax.random.permutation(key_perm, KV_HEADS)
    return (ranking < count_full).astype(jnp.int32)


def draw_w_query(key, part):
    key_noise, key_rank = jax.random.split(jax.random.fold_in(key, 7), 2)
    noise = jax.random.normal(key_noise, (D, HEADS * HEAD_DIM), jnp.float32)
    ranking = jax.random.permutation(key_rank, HEADS).astype(jnp.float32)
    strength = jnp.exp(ranking * (math.log(32.0) / (HEADS - 1)))
    column_scale = jnp.repeat(strength, HEAD_DIM)
    return (noise * column_scale[None, :] * D ** (-0.5)).astype(jnp.bfloat16)


def draw_key_cache(key, part):
    key_base, key_pick = jax.random.split(jax.random.fold_in(key, 13), 2)
    full_shape = (BATCH * BLOCKS, PAGE, KV_HEADS, HEAD_DIM)
    base = jnp.clip(jax.random.normal(key_base, full_shape, jnp.float32), -6.0, 6.0)
    rate = 16.0 / (BATCH * BLOCKS * PAGE)
    chosen = jax.random.uniform(key_pick, (BATCH * BLOCKS, PAGE, KV_HEADS, 1), jnp.float32) < rate
    strong = jnp.clip(5.0 * base, -6.0, 6.0)
    return jnp.where(chosen, strong, base).astype(jnp.bfloat16)


def with_spikes(values, stream_key, source, target, parts, factor):
    def block_of(position):
        return (jnp.arange(values.shape[position]) // (values.shape[position] // parts)).reshape((-1,) + (1,) * (values.ndim - 1 - position))

    near = jax.random.permutation(stream_key, parts)[block_of(target)]
    far = (block_of(target) + parts // 2) % parts
    return jnp.where((block_of(source) == near) | (block_of(source) == far), factor * values, values)


def shard_levels(rng, shape, pieces, low, top_value):
    level = 1.0
    for axis_at, parts in pieces:
        heights = jax.random.uniform(jax.random.fold_in(jax.random.fold_in(rng, 6), axis_at), (parts,), jnp.float32, low / len(pieces), top_value / len(pieces))
        level = level * jnp.repeat(jnp.exp(heights), shape[axis_at] // parts).reshape((-1,) + (1,) * (len(shape) - 1 - axis_at))
    return level


def normal_values(own_key, shape, scale, reach, pieces=(), held_as=jnp.bfloat16):
    factor_of = shard_levels(own_key, shape, pieces, -0.22, 0.18) if pieces else 1.0
    array = jax.random.normal(own_key, shape, jnp.float32) * scale * factor_of
    return jnp.minimum(jnp.maximum(array, -reach), reach).astype(held_as)


def bell_draw_with(rng, extent, spread, limit, shards, heavy, kind=jnp.bfloat16):
    array = spread * jax.random.normal(rng, extent, jnp.float32)
    if shards:
        array = array * shard_levels(rng, extent, shards, -0.22, 0.18)
    return jnp.clip(with_spikes(array, jax.random.fold_in(rng, 3), *heavy), -limit, limit).astype(kind)


def setup_inputs(seed: int = 0, part: int = 0) -> dict:
    streams_of = jax.random.split(jax.random.key(seed), 13)
    part_splits = jax.random.split(jax.random.fold_in(streams_of[12], part), 13)
    return {
        "hidden": normal_values(part_splits[0], (STEPS, BATCH, D), 1.0, 6.0, ((2, 16),)),
        "norm_gain": jnp.clip(1.0 + 0.1 * jax.random.normal(streams_of[1], (D,), jnp.float32), 0.5, 1.5).astype(jnp.bfloat16),
        "w_query": draw_w_query(jax.random.fold_in(streams_of[12], 71), part),
        "w_key": normal_values(streams_of[3], (D, KV_HEADS * HEAD_DIM), (D // 16) ** -0.5, 0.25, ((0, 16),)),
        "w_value": normal_values(streams_of[4], (D, KV_HEADS * HEAD_DIM), (D // 4) ** -0.5, 0.125, ((0, 16),)),
        "w_output": bell_draw_with(streams_of[5], (HEADS * HEAD_DIM, D), (HEADS * HEAD_DIM) ** -0.5, 0.09375, ((0, 16),), (0, 1, 16, 2.0)),
        "key_cache": draw_key_cache(jax.random.fold_in(jax.random.fold_in(streams_of[12], part), 71), part),
        "value_cache": normal_values(part_splits[7], (BATCH * BLOCKS, PAGE, KV_HEADS, HEAD_DIM), 1.0, 6.0, ((0, 16),)),
        "retrieval": draw_retrieval(jax.random.fold_in(streams_of[12], 71), part),
        "page_table": draw_page_table(jax.random.fold_in(jax.random.fold_in(streams_of[12], part), 71), part),
        "lengths": draw_lengths(jax.random.fold_in(jax.random.fold_in(streams_of[12], part), 71), part),
        "window_start": draw_window_start(jax.random.fold_in(jax.random.fold_in(streams_of[12], part), 71), part),
    }


very_low = -1e+30
epsilon = 1e-05

def combine(earlier, later):
    top_a, total_a, summed_a = earlier
    top_b, total_b, summed_b = later
    highest = jnp.maximum(top_a, top_b)
    factor_a = jnp.exp(top_a - highest)
    factor_b = jnp.exp(top_b - highest)
    return (highest, total_a * factor_a + total_b * factor_b, summed_a * factor_a[..., None] + summed_b * factor_b[..., None])

def arrange(top_val, total_val, summed_val, row_count):
    head_count = top_val.shape[1] * top_val.shape[2]
    top_val = jnp.transpose(top_val, (3, 0, 1, 2)).reshape(row_count, head_count)
    total_val = jnp.transpose(total_val, (3, 0, 1, 2)).reshape(row_count, head_count)
    summed_val = jnp.transpose(summed_val, (3, 0, 1, 2, 4)).reshape(row_count, head_count, summed_val.shape[-1])
    return (top_val, total_val, summed_val)

def page_partials(query_heads, page_keys, page_values, retrieval, page_table, lengths, window_start, first_page):
    page_count, page_len, kv_heads, head_dim = page_keys.shape
    batch_size, blocks = page_table.shape
    steps_n = query_heads.shape[0]
    slot_ids = first_page + jnp.arange(page_count, dtype=jnp.int32)
    matches = (page_table[None, :, :] == slot_ids[:, None, None]).astype(jnp.int32)
    owner_req = lax.optimization_barrier(jnp.sum(matches * jnp.arange(batch_size, dtype=jnp.int32)[None, :, None], axis=(1, 2)))
    block_ids = lax.optimization_barrier(jnp.sum(matches * jnp.arange(blocks, dtype=jnp.int32)[None, None, :], axis=(1, 2)))
    query_page = query_heads[:, owner_req].astype(jnp.float32)
    scores = jnp.einsum('spkgd,ptkd->pkgst', query_page, page_keys.astype(jnp.float32)) * head_dim ** (-0.5)
    positions = block_ids[:, None] * page_len + jnp.arange(page_len, dtype=jnp.int32)[None, :]
    in_range = positions < lengths[owner_req][:, None]
    recent = (positions < SINKS) | (positions >= window_start[owner_req][:, None])
    visible = in_range[:, None, :] & ((retrieval[None, :, None] == 1) | recent[:, None, :])
    visible = visible[:, :, None, None, :]
    masked = jnp.where(visible, scores, very_low)
    owner_hot = owner_req[:, None] == jnp.arange(batch_size, dtype=jnp.int32)[None, :]
    page_max = lax.optimization_barrier(jnp.max(masked, axis=-1))
    local_max = lax.optimization_barrier(jnp.max(jnp.where(owner_hot[:, :, None, None, None], page_max[:, None], very_low), axis=0))
    row_max = local_max[owner_req]
    weights = jnp.where(visible, jnp.exp(masked - row_max[..., None]), 0.0)
    owner_float = owner_hot.astype(jnp.float32)
    local_total = jnp.einsum('pb,pkgs->bkgs', owner_float, lax.optimization_barrier(jnp.sum(weights, axis=-1)), precision=lax.Precision.HIGHEST)
    rounded = weights.astype(jnp.bfloat16).astype(jnp.float32)
    values = jnp.einsum('pkgst,ptkd->pkgsd', rounded, page_values.astype(jnp.float32))
    local_sum = jnp.einsum('pb,pkgsd->bkgsd', owner_float, values, precision=lax.Precision.HIGHEST)
    return arrange(local_max, local_total, local_sum, steps_n * batch_size)

def fresh_partials(query_heads, key_heads, value_heads):
    steps_n, batch_size, kv_heads, group, head_dim = query_heads.shape
    scores = jnp.einsum('sbkgd,ubkd->bkgsu', query_heads.astype(jnp.float32), key_heads.astype(jnp.float32)) * head_dim ** (-0.5)
    causal = jnp.arange(steps_n)[:, None] >= jnp.arange(steps_n)[None, :]
    masked = jnp.where(causal, scores, very_low)
    highest = lax.optimization_barrier(jnp.max(masked, axis=-1))
    weights = jnp.where(causal, jnp.exp(masked - highest[..., None]), 0.0)
    totals = lax.optimization_barrier(jnp.sum(weights, axis=-1))
    rounded = weights.astype(jnp.bfloat16).astype(jnp.float32)
    summed = jnp.einsum('bkgsu,ubkd->bkgsd', rounded, value_heads.astype(jnp.float32))
    return arrange(highest, totals, summed, steps_n * batch_size)

def reference(hidden, norm_gain, w_query, w_key, w_value, w_output, key_cache, value_cache, retrieval, page_table, lengths, window_start):
    steps_n, batch_size, width_full = hidden.shape
    row_count = steps_n * batch_size
    floated = hidden.astype(jnp.float32)
    squares = lax.optimization_barrier(jnp.sum(floated * floated, axis=-1)).reshape(row_count, 1)
    inv_rms = lax.rsqrt(squares / D + epsilon)
    normed = (floated * norm_gain.astype(jnp.float32)).astype(jnp.bfloat16).reshape(row_count, width_full)
    query = (jnp.dot(normed, w_query, preferred_element_type=jnp.float32) * inv_rms).astype(jnp.bfloat16)
    new_key = (jnp.dot(normed, w_key, preferred_element_type=jnp.float32) * inv_rms).astype(jnp.bfloat16)
    new_value = (jnp.dot(normed, w_value, preferred_element_type=jnp.float32) * inv_rms).astype(jnp.bfloat16)
    query_heads = query.reshape(steps_n, batch_size, KV_HEADS, HEADS // KV_HEADS, HEAD_DIM)
    key_heads = new_key.reshape(steps_n, batch_size, KV_HEADS, HEAD_DIM)
    value_heads = new_value.reshape(steps_n, batch_size, KV_HEADS, HEAD_DIM)

    def visit_pages(running, group_index):
        first_page = (group_index * PAGES_DEV).astype(jnp.int32)
        page_keys = lax.dynamic_slice_in_dim(key_cache, first_page, PAGES_DEV, 0)
        page_values = lax.dynamic_slice_in_dim(value_cache, first_page, PAGES_DEV, 0)
        partial_value = page_partials(query_heads, page_keys, page_values, retrieval, page_table, lengths, window_start, first_page)
        return (combine(running, partial_value), None)
    start_state = (jnp.full((row_count, HEADS), very_low, jnp.float32), jnp.zeros((row_count, HEADS), jnp.float32), jnp.zeros((row_count, HEADS, HEAD_DIM), jnp.float32))
    running, _ = lax.scan(visit_pages, start_state, jnp.arange(N_CTX, dtype=jnp.int32))
    fresh_parts = fresh_partials(query_heads, key_heads, value_heads)
    highest, totals, summed = combine(running, fresh_parts)
    attended = (summed / totals[..., None]).reshape(row_count, HEADS * HEAD_DIM).astype(jnp.bfloat16)
    projected = jnp.dot(attended, w_output, preferred_element_type=jnp.float32).astype(jnp.bfloat16)
    return projected.reshape(steps_n, batch_size, width_full)
```

```python
import functools

import jax
import jax.numpy as jnp
from jax import lax
from jax.experimental import pallas as pl
from jax.experimental.pallas import tpu as pltpu
from jax.sharding import PartitionSpec as P

D = 8192
SINKS = 4


very_low = -1e30
epsilon = 1e-05


def merged_2(shard, axis, combine):
    everything = jax.tree.map(lambda part: lax.all_gather(part, axis), shard)
    first = jax.tree.map(lambda part: part[0], everything)

    def turn(k, so_far):
        return combine(so_far, jax.tree.map(lambda part: part[k], everything))

    return lax.fori_loop(1, lax.axis_size(axis), turn, first)


def combine(earlier, later):
    top_a, total_a, summed_a = earlier
    top_b, total_b, summed_b = later
    highest = jnp.maximum(top_a, top_b)
    factor_a = jnp.exp(top_a - highest)
    factor_b = jnp.exp(top_b - highest)
    return (
        highest,
        total_a * factor_a + total_b * factor_b,
        summed_a * factor_a[..., None] + summed_b * factor_b[..., None],
    )


def arrange(top_val, total_val, summed_val, row_count):
    head_count = top_val.shape[1] * top_val.shape[2]
    top_val = jnp.transpose(top_val, (3, 0, 1, 2)).reshape(row_count, head_count)
    total_val = jnp.transpose(total_val, (3, 0, 1, 2)).reshape(row_count, head_count)
    summed_val = jnp.transpose(summed_val, (3, 0, 1, 2, 4)).reshape(
        row_count, head_count, summed_val.shape[-1]
    )
    return (top_val, total_val, summed_val)


def page_partials(
    query_heads, page_keys, page_values, retrieval, page_table, lengths, window_start, first_page
):
    page_count, page_len, kv_heads, head_dim = page_keys.shape
    batch_size, blocks = page_table.shape
    steps_n = query_heads.shape[0]
    slot_ids = first_page + jnp.arange(page_count, dtype=jnp.int32)
    matches = (page_table[None, :, :] == slot_ids[:, None, None]).astype(jnp.int32)
    owner_req = jnp.sum(
        matches * jnp.arange(batch_size, dtype=jnp.int32)[None, :, None], axis=(1, 2)
    )
    block_ids = jnp.sum(matches * jnp.arange(blocks, dtype=jnp.int32)[None, None, :], axis=(1, 2))
    query_page = query_heads[:, owner_req]
    scores = jnp.einsum(
        "spkgd,ptkd->pkgst", query_page, page_keys, preferred_element_type=jnp.float32
    ) * head_dim ** (-0.5)
    positions = block_ids[:, None] * page_len + jnp.arange(page_len, dtype=jnp.int32)[None, :]
    in_range = positions < lengths[owner_req][:, None]
    recent = (positions < SINKS) | (positions >= window_start[owner_req][:, None])
    visible = in_range[:, None, :] & ((retrieval[None, :, None] == 1) | recent[:, None, :])
    visible = visible[:, :, None, None, :]
    masked = jnp.where(visible, scores, very_low)
    owner_hot = owner_req[:, None] == jnp.arange(batch_size, dtype=jnp.int32)[None, :]
    page_max = jnp.max(masked, axis=-1)
    local_max = jnp.max(
        jnp.where(owner_hot[:, :, None, None, None], page_max[:, None], very_low), axis=0
    )
    row_max = local_max[owner_req]
    weights = jnp.where(visible, jnp.exp(masked - row_max[..., None]), 0.0)
    owner_float = owner_hot.astype(jnp.float32)
    local_total = jnp.einsum(
        "pb,pkgs->bkgs", owner_float, jnp.sum(weights, axis=-1), precision=lax.Precision.HIGHEST
    )
    values = jnp.einsum(
        "pkgst,ptkd->pkgsd",
        weights.astype(jnp.bfloat16),
        page_values,
        preferred_element_type=jnp.float32,
    )
    local_sum = jnp.einsum("pb,pkgsd->bkgsd", owner_float, values, precision=lax.Precision.HIGHEST)
    return arrange(local_max, local_total, local_sum, steps_n * batch_size)


def fresh_partials(query_heads, key_heads, value_heads):
    steps_n, batch_size, kv_heads, group, head_dim = query_heads.shape
    scores = jnp.einsum(
        "sbkgd,ubkd->bkgsu", query_heads, key_heads, preferred_element_type=jnp.float32
    ) * head_dim ** (-0.5)
    causal = jnp.arange(steps_n)[:, None] >= jnp.arange(steps_n)[None, :]
    masked = jnp.where(causal, scores, very_low)
    highest = jnp.max(masked, axis=-1)
    weights = jnp.where(causal, jnp.exp(masked - highest[..., None]), 0.0)
    totals = jnp.sum(weights, axis=-1)
    summed = jnp.einsum(
        "bkgsu,ubkd->bkgsd",
        weights.astype(jnp.bfloat16),
        value_heads,
        preferred_element_type=jnp.float32,
    )
    return arrange(highest, totals, summed, steps_n * batch_size)


def local_small(
    hidden,
    norm_gain,
    w_query,
    w_key,
    w_value,
    w_output,
    key_cache,
    value_cache,
    retrieval,
    page_table,
    lengths,
    window_start,
):
    steps_n, batch_size, width_local = hidden.shape
    row_count = steps_n * batch_size
    page_count, page_len, kv_heads, head_dim = key_cache.shape
    query_width = w_query.shape[1]
    head_count = query_width // head_dim
    floated = hidden.astype(jnp.float32)
    squares = jnp.sum(floated * floated, axis=-1).reshape(row_count, 1)
    normed = (
        (floated * norm_gain.astype(jnp.float32))
        .astype(jnp.bfloat16)
        .reshape(row_count, width_local)
    )
    query_part = jnp.dot(normed, w_query, preferred_element_type=jnp.float32)
    key_part = jnp.dot(normed, w_key, preferred_element_type=jnp.float32)
    value_part = jnp.dot(normed, w_value, preferred_element_type=jnp.float32)
    query_sum, key_sum, value_sum, square_sum = lax.psum(
        (query_part, key_part, value_part, squares), "ctx"
    )
    inv_rms = lax.rsqrt(square_sum / D + epsilon)
    query_heads = (
        (query_sum * inv_rms)
        .astype(jnp.bfloat16)
        .reshape(steps_n, batch_size, kv_heads, head_count // kv_heads, head_dim)
    )
    key_heads = (
        (key_sum * inv_rms).astype(jnp.bfloat16).reshape(steps_n, batch_size, kv_heads, head_dim)
    )
    value_heads = (
        (value_sum * inv_rms).astype(jnp.bfloat16).reshape(steps_n, batch_size, kv_heads, head_dim)
    )
    device = lax.axis_index("ctx")
    local_parts = page_partials(
        query_heads,
        key_cache,
        value_cache,
        retrieval,
        page_table,
        lengths,
        window_start,
        device * page_count,
    )
    fresh_parts = fresh_partials(query_heads, key_heads, value_heads)
    col_share = query_width // lax.axis_size("ctx")
    col_start = device * col_share
    merged = merged_2(local_parts, "ctx", combine)
    highest, totals, summed = combine(merged, fresh_parts)
    attended_full = (
        (summed / totals[..., None]).reshape(row_count, query_width).astype(jnp.bfloat16)
    )
    attended = lax.dynamic_slice_in_dim(attended_full, col_start, col_share, 1)
    partial_out = jnp.dot(attended, w_output, preferred_element_type=jnp.float32)
    reduced = lax.psum_scatter(partial_out, "ctx", scatter_dimension=1, tiled=True)
    return reduced.reshape(steps_n, batch_size, -1).astype(jnp.bfloat16)


def swap_halves(first, second):
    low = lax.broadcasted_iota(jnp.int32, first.shape, 0) < first.shape[0] // 2
    half = first.shape[0] // 2
    return (
        jnp.where(low, first, pltpu.roll(second, half, 0)),
        jnp.where(low, pltpu.roll(first, half, 0), second),
    )


def fused(
    n,
    steps_n,
    batch,
    kv_heads,
    page_len,
    retrieval_ref,
    lengths_ref,
    window_ref,
    hidden_ref,
    gain_ref,
    table_ref,
    wq_hbm,
    wk_hbm,
    wv_hbm,
    wo_hbm,
    keys_hbm,
    values_hbm,
    out_ref,
    wq_v,
    wkv_v,
    wo_v,
    keys_v,
    values_v,
    values_t,
    msg1,
    recv1,
    gath,
    queries,
    queries_t,
    info,
    page_max,
    page_total,
    page_sum,
    msg3,
    recv3,
    msg4,
    recv4,
    wq_sem,
    wo_sem,
    wkv_sem,
    keys_sem,
    values_sem,
    send_sem,
    recv_sem,
):
    f32, bf16 = jnp.float32, jnp.bfloat16
    me = lax.axis_index("ctx")
    pages = keys_v.shape[0]
    share = wq_v.shape[2]
    width = share * n
    dim = 128
    width_local = hidden_ref.shape[1]
    scale = dim ** (-0.5)

    def peer(i):
        return lax.rem(me + i, n)

    def source(i):
        return lax.rem(me + n - i, n)

    def wq_copy(i):
        cols = pl.ds(pl.multiple_of(peer(i) * share, 128), share)
        return pltpu.make_async_copy(wq_hbm.at[:, cols], wq_v.at[i], wq_sem.at[i])

    def wo_copy(i):
        cols = pl.ds(pl.multiple_of(peer(i) * share, 128), share)
        return pltpu.make_async_copy(wo_hbm.at[:, cols], wo_v.at[i], wo_sem.at[i])

    kv_width = kv_heads * dim
    wk_copy = pltpu.make_async_copy(wk_hbm, wkv_v.at[:, pl.ds(0, kv_width)], wkv_sem.at[0])
    wv_copy = pltpu.make_async_copy(wv_hbm, wkv_v.at[:, pl.ds(kv_width, kv_width)], wkv_sem.at[1])

    def keys_copy(p):
        return pltpu.make_async_copy(keys_hbm.at[p], keys_v.at[p], keys_sem.at[p])

    def values_copy(p):
        return pltpu.make_async_copy(values_hbm.at[p], values_v.at[p], values_sem.at[p])

    def remote(phase, i, from_ref, to_ref):
        return pltpu.make_async_remote_copy(
            src_ref=from_ref,
            dst_ref=to_ref,
            send_sem=send_sem.at[phase, i],
            recv_sem=recv_sem.at[phase, i],
            device_id={"ctx": peer(i)},
            device_id_type=pl.DeviceIdType.MESH,
        )

    barrier = pltpu.get_barrier_semaphore()

    @pl.loop(1, n)
    def _(i):
        pl.semaphore_signal(
            barrier, inc=1, device_id={"ctx": peer(i)}, device_id_type=pl.DeviceIdType.MESH
        )

    wk_copy.start()
    wv_copy.start()

    @pl.loop(1, n + 1)
    def _(i):
        wq_copy(lax.rem(i, n)).start()

    @pl.loop(0, pages)
    def _(p):
        values_copy(p).start()

    @pl.loop(0, pages)
    def _(p):
        keys_copy(p).start()

    @pl.loop(1, n + 1)
    def _(i):
        wo_copy(lax.rem(i, n)).start()

    floated = hidden_ref[...].astype(f32)
    squares = jnp.sum(floated * floated, axis=1, keepdims=True)
    squares = jnp.broadcast_to(squares, (floated.shape[0], dim))
    normed = (floated * gain_ref[...].astype(f32)).astype(bf16)

    table = table_ref[...]
    page_id = lax.broadcasted_iota(jnp.int32, (pages, table.shape[1]), 0) + me * pages
    lane_block = lax.broadcasted_iota(jnp.int32, (pages, table.shape[1]), 1).astype(f32)
    owner_of = jnp.zeros((pages, 1), f32)
    base_of = jnp.zeros((pages, 1), f32)
    length_of = jnp.zeros((pages, 1), f32)
    window_of = jnp.zeros((pages, 1), f32)
    for b in range(batch):
        hit = jnp.where(table[b : b + 1, :] == page_id, 1.0, 0.0)
        found = jnp.sum(hit, axis=1, keepdims=True)
        owner_of += found * float(b)
        base_of += jnp.sum(hit * lane_block, axis=1, keepdims=True) * float(page_len)
        length_of += found * lengths_ref[b].astype(f32)
        window_of += found * window_ref[b].astype(f32)
    for row, value in enumerate((owner_of, base_of, length_of, window_of)):
        info[row] = jnp.broadcast_to(value, (pages, dim)).astype(jnp.int32)

    wk_copy.wait()
    wv_copy.wait()
    pl.semaphore_wait(barrier, n - 1)

    def project(i, to_ref):
        wq_copy(i).wait()
        cols = pl.ds(pl.multiple_of(peer(i) * dim, 128), dim)
        to_ref[:, pl.ds(0, share)] = jnp.dot(normed, wq_v[i], preferred_element_type=f32)
        to_ref[:, pl.ds(share, dim)] = jnp.dot(normed, wkv_v[:, cols], preferred_element_type=f32)
        to_ref[:, pl.ds(share + dim, dim)] = squares

    @pl.loop(1, n)
    def _(i):
        project(i, msg1.at[i])
        remote(0, i, msg1.at[i], recv1.at[me]).start()

    project(0, recv1.at[me])

    @pl.loop(0, pages)
    def _(p):
        values_copy(p).wait()
        values_t[p] = values_v[p].T

    def add_up(phase, msg, recv, acc):
        def turn(i, acc):
            remote(phase, i, msg.at[i], recv.at[source(i)]).wait_recv()
            return acc + recv[source(i)]

        return lax.fori_loop(1, n, turn, acc)

    summed = add_up(0, msg1, recv1, recv1[me])
    inv_rms = lax.rsqrt(summed[:, share + dim :] / (width_local * n) + epsilon)
    for c in range((share + dim) // dim):
        piece = summed[:, c * dim : (c + 1) * dim] * inv_rms
        gath[me, :, pl.ds(c * dim, dim)] = piece.astype(bf16).astype(f32)

    @pl.loop(1, n)
    def _(i):
        remote(1, i, gath.at[me], gath.at[me]).start()

    def spread(j):
        rows = pl.multiple_of(j * 2 * steps_n * batch, 8)
        for c in range(2):
            even = gath[j, :, pl.ds(2 * c * dim, dim)]
            odd = gath[j, :, pl.ds((2 * c + 1) * dim, dim)]
            low, high = swap_halves(even, odd)
            queries[0, pl.ds(rows + 8 * c, 8), :] = low
            queries[1, pl.ds(rows + 8 * c, 8), :] = high

    spread(me)

    @pl.loop(1, n)
    def _(i):
        remote(1, i, gath.at[me], gath.at[source(i)]).wait_recv()
        spread(source(i))

    q_rows = queries.shape[1]
    for b in range(batch):
        queries_t[b] = queries[b].T.astype(bf16)

    sub = lax.broadcasted_iota(jnp.int32, (kv_heads, dim), 0)
    lane = lax.broadcasted_iota(jnp.int32, (kv_heads, dim), 1)
    per_head = q_rows // kv_heads
    lower = sub < kv_heads // 2
    own_lane = (lane // per_head) == lax.rem(sub, kv_heads // 2)
    full_head = jnp.zeros((kv_heads, dim), jnp.int32)
    for k in range(kv_heads):
        full_head = jnp.where(sub == k, retrieval_ref[k], full_head)
    full_head = full_head == 1

    @pl.loop(0, pages)
    def _(p):
        keys_copy(p).wait()
        owner = info[0, pl.ds(p, 1), :]
        base = info[1, pl.ds(p, 1), :]
        until = jnp.where(own_lane, info[2, pl.ds(p, 1), :], 0) - base
        since = jnp.where(full_head, 0, info[3, pl.ds(p, 1), :]) - base
        sinks = SINKS - jnp.broadcast_to(base, (kv_heads, dim))
        wide_owner = jnp.concatenate([owner, owner], axis=1)
        query = jnp.where(
            wide_owner == 1, queries_t[1].astype(f32), queries_t[0].astype(f32)
        ).astype(bf16)
        scores = jnp.dot(keys_v[p], query, preferred_element_type=f32)
        scores = scores.reshape(page_len, kv_heads, q_rows)
        merged = jnp.where(lower[None], scores[:, :, :dim], scores[:, :, dim:]) * scale
        token = lax.broadcasted_iota(jnp.int32, (page_len, kv_heads, dim), 0)
        visible = (token < until[None]) & ((token >= since[None]) | (token < sinks[None]))
        masked = jnp.where(visible, merged, very_low)
        highest = jnp.max(masked, axis=0)
        weights = jnp.where(visible, jnp.exp(masked - highest[None]), 0.0)
        page_max[p] = highest
        page_total[p] = jnp.sum(weights, axis=0)
        wide = jnp.concatenate(
            [jnp.where(lower[None], weights, 0.0), jnp.where(lower[None], 0.0, weights)], axis=2
        )
        wide = wide.reshape(page_len * kv_heads, q_rows).astype(bf16)
        page_sum[p] = jnp.dot(values_t[p], wide, preferred_element_type=f32)

    def lanes_of(stat):
        kept = jnp.where(own_lane, stat, 0.0)
        return jnp.concatenate(
            [
                jnp.sum(jnp.where(lower, kept, 0.0), axis=0, keepdims=True),
                jnp.sum(jnp.where(lower, 0.0, kept), axis=0, keepdims=True),
            ],
            axis=1,
        )

    def top_turn(p, tops):
        owner = info[0, pl.ds(p, 1), :]
        return tuple(
            jnp.where(owner == b, jnp.maximum(top, page_max[p]), top) for b, top in enumerate(tops)
        )

    start = jnp.full((kv_heads, dim), very_low, f32)
    tops = lax.fori_loop(0, pages, top_turn, (start,) * batch)

    def sum_turn(p, totals):
        owner = info[0, pl.ds(p, 1), :]
        top = jnp.where(owner == 1, tops[1], tops[0])
        factor = jnp.exp(page_max[p] - top)
        term = factor * page_total[p]
        totals = tuple(total + jnp.where(owner == b, term, 0.0) for b, total in enumerate(totals))
        page_sum[p] = page_sum[p] * lanes_of(factor)
        return totals

    totals = lax.fori_loop(0, pages, sum_turn, (jnp.zeros((kv_heads, dim), f32),) * batch)

    for b in range(batch):
        acc = jnp.zeros((dim, q_rows), f32)
        for p in range(pages):
            owner = info[0, pl.ds(p, 1), :]
            wide_owner = jnp.concatenate([owner, owner], axis=1)
            acc += jnp.where(wide_owner == b, page_sum[p], 0.0)
        msg3[:, pl.ds(16 * b, 16), :] = acc.T.reshape(n, q_rows // n, dim)
    stats = []
    for b in range(batch):
        for stat in (tops[b], totals[b]):
            stats.append(jnp.broadcast_to(lanes_of(stat), (dim // 4, q_rows)))
    msg3[:, pl.ds(32, 16), :] = jnp.concatenate(stats, axis=0).T.reshape(n, q_rows // n, dim)

    @pl.loop(1, n)
    def _(i):
        remote(2, i, msg3.at[peer(i)], recv3.at[me]).start()

    recv3[me] = msg3[me]

    mine = pl.ds(pl.multiple_of(me * 16, 8), 16)
    own_query = jnp.concatenate([queries[b, mine, :] for b in range(batch)], axis=0)
    head = me // 2
    new_key = gath[head, :, pl.ds(share, dim)]
    new_value = gath[kv_heads + head, :, pl.ds(share, dim)]
    fresh = (
        lax.dot_general(
            own_query, new_key, (((1,), (1,)), ((), ())), preferred_element_type=f32
        )
        * scale
    )
    row = lax.broadcasted_iota(jnp.int32, fresh.shape, 0)
    col = lax.broadcasted_iota(jnp.int32, fresh.shape, 1)
    causal = (row // 16 == col // steps_n) & (lax.rem(row, steps_n) >= lax.rem(col, steps_n))
    fresh = jnp.where(causal, fresh, very_low)
    fresh_max = jnp.max(fresh, axis=1, keepdims=True)
    fresh_weights = jnp.where(causal, jnp.exp(fresh - fresh_max), 0.0)
    fresh_total = jnp.sum(fresh_weights, axis=1, keepdims=True)
    fresh_sum = jnp.dot(
        fresh_weights.astype(bf16).astype(f32), new_value, preferred_element_type=f32
    )

    @pl.loop(1, n)
    def _(i):
        remote(2, i, msg3.at[peer(i)], recv3.at[source(i)]).wait_recv()

    top = lax.fori_loop(
        0,
        n,
        lambda j, top: jnp.maximum(top, recv3[j, pl.ds(32, 16), :]),
        jnp.full((16, dim), very_low, f32),
    )
    attended = []
    for b in range(batch):
        rows = slice(16 * b, 16 * b + 16)
        highest = jnp.maximum(top[:, 64 * b : 64 * b + 1], fresh_max[rows])
        factor = jnp.exp(fresh_max[rows] - highest)
        total = fresh_total[rows] * factor
        acc = fresh_sum[rows] * factor

        def merge_turn(j, state, b=b, highest=highest):
            total, acc = state
            stat = recv3[j, pl.ds(32, 16), :]
            factor = jnp.exp(stat[:, 64 * b : 64 * b + 1] - highest)
            total = total + stat[:, 64 * b + 32 : 64 * b + 33] * factor
            return total, acc + recv3[j, pl.ds(16 * b, 16), :] * factor

        total, acc = lax.fori_loop(0, n, merge_turn, (total, acc))
        attended.append(acc / total)
    first = swap_halves(attended[0][:8], attended[1][:8])
    second = swap_halves(attended[0][8:], attended[1][8:])
    attended = jnp.concatenate(first + second, axis=1).astype(bf16)

    def project_out(i):
        wo_copy(i).wait()
        return jnp.dot(attended, wo_v[i], preferred_element_type=f32)

    @pl.loop(1, n)
    def _(i):
        msg4[i] = project_out(i)
        remote(3, i, msg4.at[i], recv4.at[me]).start()

    out_ref[...] = add_up(3, msg4, recv4, project_out(0))

    @pl.loop(1, n)
    def _(i):
        remote(0, i, msg1.at[i], recv1.at[me]).wait_send()
        remote(1, i, gath.at[me], gath.at[me]).wait_send()
        remote(2, i, msg3.at[peer(i)], recv3.at[me]).wait_send()
        remote(3, i, msg4.at[i], recv4.at[me]).wait_send()


def local(
    hidden,
    norm_gain,
    w_query,
    w_key,
    w_value,
    w_output,
    key_cache,
    value_cache,
    retrieval,
    page_table,
    lengths,
    window_start,
):
    n = lax.axis_size("ctx")
    steps_n, batch, width_local = hidden.shape
    pages, page_len, kv_heads, dim = key_cache.shape
    query_width = w_query.shape[1]
    share = query_width // n
    rows = steps_n * batch
    q_rows = query_width // dim * steps_n
    if (n, share, rows, batch, kv_heads, dim) != (2 * kv_heads, 4 * dim, 8, 2, 8, 128):
        return local_small(
            hidden,
            norm_gain,
            w_query,
            w_key,
            w_value,
            w_output,
            key_cache,
            value_cache,
            retrieval,
            page_table,
            lengths,
            window_start,
        )
    f32, bf16 = jnp.float32, jnp.bfloat16
    smem = pl.BlockSpec(memory_space=pltpu.SMEM)
    vmem = pl.BlockSpec(memory_space=pltpu.VMEM)
    hbm = pl.BlockSpec(memory_space=pl.ANY)
    dma = pltpu.SemaphoreType.DMA
    out = pl.pallas_call(
        functools.partial(fused, n, steps_n, batch, kv_heads, page_len),
        out_shape=jax.ShapeDtypeStruct((rows, w_output.shape[1] // n), f32),
        in_specs=[smem] * 3 + [vmem] * 3 + [hbm] * 6,
        out_specs=vmem,
        scratch_shapes=[
            pltpu.VMEM((n, width_local, share), bf16),
            pltpu.VMEM((width_local, 2 * kv_heads * dim), bf16),
            pltpu.VMEM((n, share, w_output.shape[1] // n), bf16),
            pltpu.VMEM((pages, page_len * kv_heads, dim), bf16),
            pltpu.VMEM((pages, page_len * kv_heads, dim), bf16),
            pltpu.VMEM((pages, dim, page_len * kv_heads), bf16),
            pltpu.VMEM((n, rows, share + 2 * dim), f32),
            pltpu.VMEM((n, rows, share + 2 * dim), f32),
            pltpu.VMEM((n, rows, share + dim), f32),
            pltpu.VMEM((batch, q_rows, dim), f32),
            pltpu.VMEM((batch, dim, q_rows), bf16),
            pltpu.VMEM((4, pages, dim), jnp.int32),
            pltpu.VMEM((pages, kv_heads, dim), f32),
            pltpu.VMEM((pages, kv_heads, dim), f32),
            pltpu.VMEM((pages, dim, q_rows), f32),
            pltpu.VMEM((n, 48, dim), f32),
            pltpu.VMEM((n, 48, dim), f32),
            pltpu.VMEM((n, rows, share), f32),
            pltpu.VMEM((n, rows, share), f32),
            dma((n,)),
            dma((n,)),
            dma((2,)),
            dma((pages,)),
            dma((pages,)),
            dma((4, n)),
            dma((4, n)),
        ],
        compiler_params=pltpu.CompilerParams(
            collective_id=0, has_side_effects=True, vmem_limit_bytes=56 * 2**20
        ),
    )(
        retrieval,
        lengths,
        window_start,
        jnp.transpose(hidden, (1, 0, 2)).reshape(rows, width_local),
        norm_gain.reshape(1, width_local),
        page_table,
        w_query,
        w_key,
        w_value,
        w_output,
        key_cache.reshape(pages, page_len * kv_heads, dim),
        value_cache.reshape(pages, page_len * kv_heads, dim),
    )
    out = out.reshape(batch, steps_n, out.shape[1])
    return jnp.transpose(out, (1, 0, 2)).astype(bf16)


def solution(mesh):
    placed = (
        P(None, "groups", "ctx"),
        P("ctx"),
        P("ctx", None),
        P("ctx", None),
        P("ctx", None),
        P("ctx", None),
        P(("groups", "ctx"), None, None, None),
        P(("groups", "ctx"), None, None, None),
        P(),
        P("groups", None),
        P("groups"),
        P("groups"),
    )
    return jax.shard_map(
        local, mesh=mesh, in_specs=placed, out_specs=P(None, "groups", "ctx"), check_vma=False
    )
```

```python
import functools

import jax
import jax.numpy as jnp
from jax import lax
from jax.experimental import pallas as pl
from jax.experimental.pallas import tpu as pltpu
from jax.sharding import PartitionSpec as P

D = 8192
SINKS = 4


very_low = -1e30
epsilon = 1e-05


def merged_2(shard, axis, combine):
    everything = jax.tree.map(lambda part: lax.all_gather(part, axis), shard)
    first = jax.tree.map(lambda part: part[0], everything)

    def turn(k, so_far):
        return combine(so_far, jax.tree.map(lambda part: part[k], everything))

    return lax.fori_loop(1, lax.axis_size(axis), turn, first)


def combine(earlier, later):
    top_a, total_a, summed_a = earlier
    top_b, total_b, summed_b = later
    highest = jnp.maximum(top_a, top_b)
    factor_a = jnp.exp(top_a - highest)
    factor_b = jnp.exp(top_b - highest)
    return (
        highest,
        total_a * factor_a + total_b * factor_b,
        summed_a * factor_a[..., None] + summed_b * factor_b[..., None],
    )


def arrange(top_val, total_val, summed_val, row_count):
    head_count = top_val.shape[1] * top_val.shape[2]
    top_val = jnp.transpose(top_val, (3, 0, 1, 2)).reshape(row_count, head_count)
    total_val = jnp.transpose(total_val, (3, 0, 1, 2)).reshape(row_count, head_count)
    summed_val = jnp.transpose(summed_val, (3, 0, 1, 2, 4)).reshape(
        row_count, head_count, summed_val.shape[-1]
    )
    return (top_val, total_val, summed_val)


def page_partials(
    query_heads, page_keys, page_values, retrieval, page_table, lengths, window_start, first_page
):
    page_count, page_len, kv_heads, head_dim = page_keys.shape
    batch_size, blocks = page_table.shape
    steps_n = query_heads.shape[0]
    slot_ids = first_page + jnp.arange(page_count, dtype=jnp.int32)
    matches = (page_table[None, :, :] == slot_ids[:, None, None]).astype(jnp.int32)
    owner_req = jnp.sum(
        matches * jnp.arange(batch_size, dtype=jnp.int32)[None, :, None], axis=(1, 2)
    )
    block_ids = jnp.sum(matches * jnp.arange(blocks, dtype=jnp.int32)[None, None, :], axis=(1, 2))
    query_page = query_heads[:, owner_req]
    scores = jnp.einsum(
        "spkgd,ptkd->pkgst", query_page, page_keys, preferred_element_type=jnp.float32
    ) * head_dim ** (-0.5)
    positions = block_ids[:, None] * page_len + jnp.arange(page_len, dtype=jnp.int32)[None, :]
    in_range = positions < lengths[owner_req][:, None]
    recent = (positions < SINKS) | (positions >= window_start[owner_req][:, None])
    visible = in_range[:, None, :] & ((retrieval[None, :, None] == 1) | recent[:, None, :])
    visible = visible[:, :, None, None, :]
    masked = jnp.where(visible, scores, very_low)
    owner_hot = owner_req[:, None] == jnp.arange(batch_size, dtype=jnp.int32)[None, :]
    page_max = jnp.max(masked, axis=-1)
    local_max = jnp.max(
        jnp.where(owner_hot[:, :, None, None, None], page_max[:, None], very_low), axis=0
    )
    row_max = local_max[owner_req]
    weights = jnp.where(visible, jnp.exp(masked - row_max[..., None]), 0.0)
    owner_float = owner_hot.astype(jnp.float32)
    local_total = jnp.einsum(
        "pb,pkgs->bkgs", owner_float, jnp.sum(weights, axis=-1), precision=lax.Precision.HIGHEST
    )
    values = jnp.einsum(
        "pkgst,ptkd->pkgsd",
        weights.astype(jnp.bfloat16),
        page_values,
        preferred_element_type=jnp.float32,
    )
    local_sum = jnp.einsum("pb,pkgsd->bkgsd", owner_float, values, precision=lax.Precision.HIGHEST)
    return arrange(local_max, local_total, local_sum, steps_n * batch_size)


def fresh_partials(query_heads, key_heads, value_heads):
    steps_n, batch_size, kv_heads, group, head_dim = query_heads.shape
    scores = jnp.einsum(
        "sbkgd,ubkd->bkgsu", query_heads, key_heads, preferred_element_type=jnp.float32
    ) * head_dim ** (-0.5)
    causal = jnp.arange(steps_n)[:, None] >= jnp.arange(steps_n)[None, :]
    masked = jnp.where(causal, scores, very_low)
    highest = jnp.max(masked, axis=-1)
    weights = jnp.where(causal, jnp.exp(masked - highest[..., None]), 0.0)
    totals = jnp.sum(weights, axis=-1)
    summed = jnp.einsum(
        "bkgsu,ubkd->bkgsd",
        weights.astype(jnp.bfloat16),
        value_heads,
        preferred_element_type=jnp.float32,
    )
    return arrange(highest, totals, summed, steps_n * batch_size)


def local_small(
    hidden,
    norm_gain,
    w_query,
    w_key,
    w_value,
    w_output,
    key_cache,
    value_cache,
    retrieval,
    page_table,
    lengths,
    window_start,
):
    steps_n, batch_size, width_local = hidden.shape
    row_count = steps_n * batch_size
    page_count, page_len, kv_heads, head_dim = key_cache.shape
    query_width = w_query.shape[1]
    head_count = query_width // head_dim
    floated = hidden.astype(jnp.float32)
    squares = jnp.sum(floated * floated, axis=-1).reshape(row_count, 1)
    normed = (
        (floated * norm_gain.astype(jnp.float32))
        .astype(jnp.bfloat16)
        .reshape(row_count, width_local)
    )
    query_part = jnp.dot(normed, w_query, preferred_element_type=jnp.float32)
    key_part = jnp.dot(normed, w_key, preferred_element_type=jnp.float32)
    value_part = jnp.dot(normed, w_value, preferred_element_type=jnp.float32)
    query_sum, key_sum, value_sum, square_sum = lax.psum(
        (query_part, key_part, value_part, squares), "ctx"
    )
    inv_rms = lax.rsqrt(square_sum / D + epsilon)
    query_heads = (
        (query_sum * inv_rms)
        .astype(jnp.bfloat16)
        .reshape(steps_n, batch_size, kv_heads, head_count // kv_heads, head_dim)
    )
    key_heads = (
        (key_sum * inv_rms).astype(jnp.bfloat16).reshape(steps_n, batch_size, kv_heads, head_dim)
    )
    value_heads = (
        (value_sum * inv_rms).astype(jnp.bfloat16).reshape(steps_n, batch_size, kv_heads, head_dim)
    )
    device = lax.axis_index("ctx")
    local_parts = page_partials(
        query_heads,
        key_cache,
        value_cache,
        retrieval,
        page_table,
        lengths,
        window_start,
        device * page_count,
    )
    fresh_parts = fresh_partials(query_heads, key_heads, value_heads)
    col_share = query_width // lax.axis_size("ctx")
    col_start = device * col_share
    merged = merged_2(local_parts, "ctx", combine)
    highest, totals, summed = combine(merged, fresh_parts)
    attended_full = (
        (summed / totals[..., None]).reshape(row_count, query_width).astype(jnp.bfloat16)
    )
    attended = lax.dynamic_slice_in_dim(attended_full, col_start, col_share, 1)
    partial_out = jnp.dot(attended, w_output, preferred_element_type=jnp.float32)
    reduced = lax.psum_scatter(partial_out, "ctx", scatter_dimension=1, tiled=True)
    return reduced.reshape(steps_n, batch_size, -1).astype(jnp.bfloat16)


def swap_halves(first, second):
    low = lax.broadcasted_iota(jnp.int32, first.shape, 0) < first.shape[0] // 2
    half = first.shape[0] // 2
    return (
        jnp.where(low, first, pltpu.roll(second, half, 0)),
        jnp.where(low, pltpu.roll(first, half, 0), second),
    )


def fused(
    n,
    steps_n,
    batch,
    kv_heads,
    page_len,
    retrieval_ref,
    lengths_ref,
    window_ref,
    hidden_ref,
    gain_ref,
    table_ref,
    wq_hbm,
    wk_hbm,
    wv_hbm,
    wo_hbm,
    keys_hbm,
    values_hbm,
    out_ref,
    wq_v,
    wkv_v,
    wo_v,
    keys_v,
    values_v,
    values_t,
    msg1,
    recv1,
    gath,
    queries,
    queries_t,
    info,
    owners,
    page_max,
    page_total,
    page_sum,
    msg3,
    recv3,
    msg4,
    recv4,
    wq_sem,
    wo_sem,
    wkv_sem,
    keys_sem,
    values_sem,
    send_sem,
    recv_sem,
):
    f32, bf16 = jnp.float32, jnp.bfloat16
    me = lax.axis_index("ctx")
    pages = keys_v.shape[0]
    share = wq_v.shape[2]
    width = share * n
    dim = 128
    width_local = hidden_ref.shape[2]
    scale = dim ** (-0.5)

    def peer(i):
        return lax.rem(me + i, n)

    def source(i):
        return lax.rem(me + n - i, n)

    def wq_copy(i):
        cols = pl.ds(pl.multiple_of(peer(i) * share, 128), share)
        return pltpu.make_async_copy(wq_hbm.at[:, cols], wq_v.at[i], wq_sem.at[i])

    def wo_copy(i):
        cols = pl.ds(pl.multiple_of(peer(i) * share, 128), share)
        return pltpu.make_async_copy(wo_hbm.at[:, cols], wo_v.at[i], wo_sem.at[i])

    kv_width = kv_heads * dim
    wk_copy = pltpu.make_async_copy(wk_hbm, wkv_v.at[:, pl.ds(0, kv_width)], wkv_sem.at[0])
    wv_copy = pltpu.make_async_copy(wv_hbm, wkv_v.at[:, pl.ds(kv_width, kv_width)], wkv_sem.at[1])

    def keys_copy(p):
        return pltpu.make_async_copy(keys_hbm.at[p], keys_v.at[p], keys_sem.at[p])

    def values_copy(p):
        return pltpu.make_async_copy(values_hbm.at[p], values_v.at[p], values_sem.at[p])

    def remote(phase, i, from_ref, to_ref):
        return pltpu.make_async_remote_copy(
            src_ref=from_ref,
            dst_ref=to_ref,
            send_sem=send_sem.at[phase, i],
            recv_sem=recv_sem.at[phase, i],
            device_id={"ctx": peer(i)},
            device_id_type=pl.DeviceIdType.MESH,
        )

    barrier = pltpu.get_barrier_semaphore()

    @pl.loop(1, n)
    def _(i):
        pl.semaphore_signal(
            barrier, inc=1, device_id={"ctx": peer(i)}, device_id_type=pl.DeviceIdType.MESH
        )

    wk_copy.start()
    wv_copy.start()

    @pl.loop(1, n + 1)
    def _(i):
        wq_copy(lax.rem(i, n)).start()

    @pl.loop(0, pages)
    def _(p):
        values_copy(p).start()

    @pl.loop(0, pages)
    def _(p):
        keys_copy(p).start()

    @pl.loop(1, n + 1)
    def _(i):
        wo_copy(lax.rem(i, n)).start()

    loaded = hidden_ref[...].astype(f32)
    floated = jnp.concatenate(
        [loaded[s, b : b + 1, :] for b in range(batch) for s in range(steps_n)], axis=0
    )
    squares = jnp.sum(floated * floated, axis=1, keepdims=True)
    squares = jnp.broadcast_to(squares, (floated.shape[0], dim))
    normed = (floated * gain_ref[...].astype(f32).reshape(1, width_local)).astype(bf16)

    table = table_ref[...]
    page_id = lax.broadcasted_iota(jnp.int32, (pages, table.shape[1]), 0) + me * pages
    lane_block = lax.broadcasted_iota(jnp.int32, (pages, table.shape[1]), 1).astype(f32)
    owner_of = jnp.zeros((pages, 1), f32)
    base_of = jnp.zeros((pages, 1), f32)
    length_of = jnp.zeros((pages, 1), f32)
    window_of = jnp.zeros((pages, 1), f32)
    for b in range(batch):
        hit = jnp.where(table[b : b + 1, :] == page_id, 1.0, 0.0)
        found = jnp.sum(hit, axis=1, keepdims=True)
        owner_of += found * float(b)
        base_of += jnp.sum(hit * lane_block, axis=1, keepdims=True) * float(page_len)
        length_of += found * lengths_ref[b].astype(f32)
        window_of += found * window_ref[b].astype(f32)
    for row, value in enumerate((owner_of, base_of, length_of, window_of)):
        info[row] = jnp.broadcast_to(value, (pages, dim)).astype(jnp.int32)

    @pl.loop(0, pages)
    def _(p):
        found = jnp.sum(jnp.where(table[1:2, :] == me * pages + p, 1, 0))
        owners[p] = jnp.minimum(found, batch - 1)

    wk_copy.wait()
    wv_copy.wait()
    pl.semaphore_wait(barrier, n - 1)

    def project(i, to_ref):
        wq_copy(i).wait()
        cols = pl.ds(pl.multiple_of(peer(i) * dim, 128), dim)
        to_ref[:, pl.ds(0, share)] = jnp.dot(normed, wq_v[i], preferred_element_type=f32)
        to_ref[:, pl.ds(share, dim)] = jnp.dot(normed, wkv_v[:, cols], preferred_element_type=f32)
        to_ref[:, pl.ds(share + dim, dim)] = squares

    @pl.loop(1, n)
    def _(i):
        project(i, msg1.at[i])
        remote(0, i, msg1.at[i], recv1.at[me]).start()

    project(0, recv1.at[me])

    @pl.loop(0, pages)
    def _(p):
        values_copy(p).wait()
        values_t[p] = values_v[p].T

    def add_up(phase, msg, recv, acc):
        def turn(i, acc):
            remote(phase, i, msg.at[i], recv.at[source(i)]).wait_recv()
            return acc + recv[source(i)]

        return lax.fori_loop(1, n, turn, acc)

    summed = add_up(0, msg1, recv1, recv1[me])
    inv_rms = lax.rsqrt(summed[:, share + dim :] / (width_local * n) + epsilon)
    for c in range((share + dim) // dim):
        piece = summed[:, c * dim : (c + 1) * dim] * inv_rms
        gath[me, :, pl.ds(c * dim, dim)] = piece.astype(bf16).astype(f32)

    @pl.loop(1, n)
    def _(i):
        remote(1, i, gath.at[me], gath.at[me]).start()

    def spread(j):
        rows = pl.multiple_of(j * 2 * steps_n * batch, 8)
        for c in range(2):
            even = gath[j, :, pl.ds(2 * c * dim, dim)]
            odd = gath[j, :, pl.ds((2 * c + 1) * dim, dim)]
            low, high = swap_halves(even, odd)
            queries[0, pl.ds(rows + 8 * c, 8), :] = low
            queries[1, pl.ds(rows + 8 * c, 8), :] = high

    spread(me)

    @pl.loop(1, n)
    def _(i):
        remote(1, i, gath.at[me], gath.at[source(i)]).wait_recv()
        spread(source(i))

    q_rows = queries.shape[1]
    per_head = q_rows // kv_heads
    groups = dim // per_head
    part = page_len // groups
    for b in range(batch):
        turned = queries[b].T
        for i in range(groups):
            queries_t[b, i] = jnp.concatenate(
                [
                    pltpu.roll(turned[:, :dim], per_head * i, 1),
                    pltpu.roll(turned[:, dim:], per_head * i, 1),
                ],
                axis=1,
            ).astype(bf16)

    sub = lax.broadcasted_iota(jnp.int32, (kv_heads, dim), 0)
    lane = lax.broadcasted_iota(jnp.int32, (kv_heads, dim), 1)
    lower = sub < kv_heads // 2
    group = lax.rem(lane // per_head - lax.rem(sub, groups) + groups, groups)
    own_lane = group == 0
    full_head = jnp.zeros((kv_heads, dim), jnp.int32)
    for k in range(kv_heads):
        full_head = jnp.where(sub == k, retrieval_ref[k], full_head)
    full_head = full_head == 1

    @pl.loop(0, pages)
    def _(p):
        keys_copy(p).wait()
        base = info[1, pl.ds(p, 1), :] + part * group
        until = info[2, pl.ds(p, 1), :] - base
        since = jnp.where(full_head, 0, info[3, pl.ds(p, 1), :]) - base
        sinks = SINKS - base
        merged = None
        for i in range(groups):
            rows = pl.ds(i * part * kv_heads, part * kv_heads)
            scores = jnp.dot(keys_v[p, rows, :], queries_t[owners[p], i], preferred_element_type=f32)
            scores = scores.reshape(part, kv_heads, q_rows)
            scores = jnp.where(lower[None], scores[:, :, :dim], scores[:, :, dim:])
            merged = scores if i == 0 else jnp.where((group == i)[None], scores, merged)
        token = lax.broadcasted_iota(jnp.int32, (part, kv_heads, dim), 0)
        visible = (token < until[None]) & ((token >= since[None]) | (token < sinks[None]))
        masked = jnp.where(visible, merged * scale, very_low)
        highest = jnp.max(masked, axis=0)
        for shift in range(groups.bit_length() - 1):
            highest = jnp.maximum(highest, pltpu.roll(highest, per_head << shift, 1))
        weights = jnp.where(visible, jnp.exp(masked - highest[None]), 0.0)
        total = jnp.sum(weights, axis=0)
        for shift in range(groups.bit_length() - 1):
            total = total + pltpu.roll(total, per_head << shift, 1)
        page_max[p] = highest
        page_total[p] = total
        wide = []
        for i in range(groups):
            turned = weights if i == 0 else pltpu.roll(weights, dim - per_head * i, 2)
            both = jnp.concatenate(
                [
                    jnp.where((own_lane & lower)[None], turned, 0.0),
                    jnp.where((own_lane & ~lower)[None], turned, 0.0),
                ],
                axis=2,
            )
            wide.append(both.reshape(part * kv_heads, q_rows).astype(bf16))
        page_sum[p] = jnp.dot(
            values_t[p], jnp.concatenate(wide, axis=0), preferred_element_type=f32
        )

    def lanes_of(stat):
        kept = jnp.where(own_lane, stat, 0.0)
        return jnp.concatenate(
            [
                jnp.sum(jnp.where(lower, kept, 0.0), axis=0, keepdims=True),
                jnp.sum(jnp.where(lower, 0.0, kept), axis=0, keepdims=True),
            ],
            axis=1,
        )

    def top_turn(p, tops):
        owner = info[0, pl.ds(p, 1), :]
        return tuple(
            jnp.where(owner == b, jnp.maximum(top, page_max[p]), top) for b, top in enumerate(tops)
        )

    start = jnp.full((kv_heads, dim), very_low, f32)
    tops = lax.fori_loop(0, pages, top_turn, (start,) * batch)

    def sum_turn(p, totals):
        owner = info[0, pl.ds(p, 1), :]
        top = jnp.where(owner == 1, tops[1], tops[0])
        factor = jnp.exp(page_max[p] - top)
        term = factor * page_total[p]
        totals = tuple(total + jnp.where(owner == b, term, 0.0) for b, total in enumerate(totals))
        page_sum[p] = page_sum[p] * lanes_of(factor)
        return totals

    totals = lax.fori_loop(0, pages, sum_turn, (jnp.zeros((kv_heads, dim), f32),) * batch)

    for b in range(batch):
        acc = jnp.zeros((dim, q_rows), f32)
        for p in range(pages):
            owner = info[0, pl.ds(p, 1), :]
            wide_owner = jnp.concatenate([owner, owner], axis=1)
            acc += jnp.where(wide_owner == b, page_sum[p], 0.0)
        msg3[:, pl.ds(16 * b, 16), :] = acc.T.reshape(n, q_rows // n, dim)
    stats = jnp.concatenate(
        [lanes_of(tops[0]), lanes_of(tops[1]), lanes_of(totals[0]), lanes_of(totals[1])]
        + [jnp.zeros((4, q_rows), f32)],
        axis=0,
    )
    span = q_rows // n
    for j in range(n):
        at = j * span // dim * dim
        moved = (dim - (j * span - at)) % dim
        piece = stats[:, at : at + dim]
        msg3[j, pl.ds(32, 8), :] = piece if moved == 0 else pltpu.roll(piece, moved, 1)

    @pl.loop(1, n)
    def _(i):
        remote(2, i, msg3.at[peer(i)], recv3.at[me]).start()

    recv3[me] = msg3[me]

    mine = pl.ds(pl.multiple_of(me * 16, 8), 16)
    head = me // 2
    new_key = gath[head, :, pl.ds(share, dim)]
    new_value = gath[kv_heads + head, :, pl.ds(share, dim)]
    row = lax.broadcasted_iota(jnp.int32, (8, dim), 0)
    col = lax.broadcasted_iota(jnp.int32, (8, dim), 1)
    fresh_max = jnp.full((8, dim), very_low, f32)
    fresh_total = jnp.zeros((8, dim), f32)
    fresh_sum = []
    for b in range(batch):
        own_query = jnp.concatenate([queries[b, mine, :]] * (dim // 16), axis=0)
        fresh = lax.dot_general(
            new_key, own_query, (((1,), (1,)), ((), ())), preferred_element_type=f32
        )
        causal = (row // steps_n == b) & (lax.rem(row, steps_n) <= lax.rem(col, steps_n))
        fresh = jnp.where(causal, fresh * scale, very_low)
        highest = jnp.max(fresh, axis=0, keepdims=True)
        weights = jnp.where(causal, jnp.exp(fresh - highest), 0.0)
        fresh_max = jnp.where(row == b, highest, fresh_max)
        fresh_total = jnp.where(row == b, jnp.sum(weights, axis=0, keepdims=True), fresh_total)
        fresh_sum.append(
            lax.dot_general(
                weights.astype(bf16).astype(f32),
                new_value,
                (((0,), (0,)), ((), ())),
                preferred_element_type=f32,
            )[:16]
        )

    @pl.loop(1, n)
    def _(i):
        remote(2, i, msg3.at[peer(i)], recv3.at[source(i)]).wait_recv()

    parts = recv3[:, pl.ds(32, 8), :]
    top = jnp.maximum(jnp.max(parts, axis=0), fresh_max)
    factor = jnp.exp(parts - top[None])
    fresh_factor = jnp.exp(fresh_max - top)
    total = jnp.sum(factor * pltpu.roll(parts, 8 - batch, 1), axis=0) + fresh_factor * fresh_total
    total = jnp.where(row < batch, total, 1.0)
    factor = factor / total[None]
    fresh_factor = pltpu.roll(fresh_factor / total, 4, 0)
    factor = jnp.where((row < 4)[None], factor, fresh_factor[None]).reshape(n * 8, dim).T[:16]
    attended = []
    for b in range(batch):
        acc = fresh_sum[b] * factor[:, 4 + b : 5 + b]
        for j in range(n):
            acc += recv3[j, pl.ds(16 * b, 16), :] * factor[:, 8 * j + b : 8 * j + b + 1]
        attended.append(acc)
    first = swap_halves(attended[0][:8], attended[1][:8])
    second = swap_halves(attended[0][8:], attended[1][8:])
    attended = jnp.concatenate(first + second, axis=1).astype(bf16)

    def project_out(i):
        wo_copy(i).wait()
        return jnp.dot(attended, wo_v[i], preferred_element_type=f32)

    @pl.loop(1, n)
    def _(i):
        msg4[i] = project_out(i)
        remote(3, i, msg4.at[i], recv4.at[me]).start()

    result = add_up(3, msg4, recv4, project_out(0))
    for s in range(steps_n):
        out_ref[s] = jnp.concatenate(
            [result[b * steps_n + s : b * steps_n + s + 1] for b in range(batch)], axis=0
        ).astype(out_ref.dtype)

    @pl.loop(1, n)
    def _(i):
        remote(0, i, msg1.at[i], recv1.at[me]).wait_send()
        remote(1, i, gath.at[me], gath.at[me]).wait_send()
        remote(2, i, msg3.at[peer(i)], recv3.at[me]).wait_send()
        remote(3, i, msg4.at[i], recv4.at[me]).wait_send()


def local(
    hidden,
    norm_gain,
    w_query,
    w_key,
    w_value,
    w_output,
    key_cache,
    value_cache,
    retrieval,
    page_table,
    lengths,
    window_start,
):
    n = lax.axis_size("ctx")
    steps_n, batch, width_local = hidden.shape
    pages, page_len, kv_heads, dim = key_cache.shape
    query_width = w_query.shape[1]
    share = query_width // n
    rows = steps_n * batch
    q_rows = query_width // dim * steps_n
    if (n, share, rows, batch, kv_heads, dim) != (2 * kv_heads, 4 * dim, 8, 2, 8, 128):
        return local_small(
            hidden,
            norm_gain,
            w_query,
            w_key,
            w_value,
            w_output,
            key_cache,
            value_cache,
            retrieval,
            page_table,
            lengths,
            window_start,
        )
    f32, bf16 = jnp.float32, jnp.bfloat16
    smem = pl.BlockSpec(memory_space=pltpu.SMEM)
    vmem = pl.BlockSpec(memory_space=pltpu.VMEM)
    hbm = pl.BlockSpec(memory_space=pl.ANY)
    dma = pltpu.SemaphoreType.DMA
    out = pl.pallas_call(
        functools.partial(fused, n, steps_n, batch, kv_heads, page_len),
        out_shape=jax.ShapeDtypeStruct((steps_n, batch, w_output.shape[1] // n), bf16),
        in_specs=[smem] * 3 + [vmem] * 3 + [hbm] * 6,
        out_specs=vmem,
        scratch_shapes=[
            pltpu.VMEM((n, width_local, share), bf16),
            pltpu.VMEM((width_local, 2 * kv_heads * dim), bf16),
            pltpu.VMEM((n, share, w_output.shape[1] // n), bf16),
            pltpu.VMEM((pages, page_len * kv_heads, dim), bf16),
            pltpu.VMEM((pages, page_len * kv_heads, dim), bf16),
            pltpu.VMEM((pages, dim, page_len * kv_heads), bf16),
            pltpu.VMEM((n, rows, share + 2 * dim), f32),
            pltpu.VMEM((n, rows, share + 2 * dim), f32),
            pltpu.VMEM((n, rows, share + dim), f32),
            pltpu.VMEM((batch, q_rows, dim), f32),
            pltpu.VMEM((batch, dim // (q_rows // kv_heads), dim, q_rows), bf16),
            pltpu.VMEM((4, pages, dim), jnp.int32),
            pltpu.SMEM((pages,), jnp.int32),
            pltpu.VMEM((pages, kv_heads, dim), f32),
            pltpu.VMEM((pages, kv_heads, dim), f32),
            pltpu.VMEM((pages, dim, q_rows), f32),
            pltpu.VMEM((n, 40, dim), f32),
            pltpu.VMEM((n, 40, dim), f32),
            pltpu.VMEM((n, rows, share), f32),
            pltpu.VMEM((n, rows, share), f32),
            dma((n,)),
            dma((n,)),
            dma((2,)),
            dma((pages,)),
            dma((pages,)),
            dma((4, n)),
            dma((4, n)),
        ],
        compiler_params=pltpu.CompilerParams(
            collective_id=0, has_side_effects=True, vmem_limit_bytes=56 * 2**20
        ),
    )(
        retrieval,
        lengths,
        window_start,
        hidden,
        norm_gain,
        page_table,
        w_query,
        w_key,
        w_value,
        w_output,
        key_cache.reshape(pages, page_len * kv_heads, dim),
        value_cache.reshape(pages, page_len * kv_heads, dim),
    )
    return out


def solution(mesh):
    placed = (
        P(None, "groups", "ctx"),
        P("ctx"),
        P("ctx", None),
        P("ctx", None),
        P("ctx", None),
        P("ctx", None),
        P(("groups", "ctx"), None, None, None),
        P(("groups", "ctx"), None, None, None),
        P(),
        P("groups", None),
        P("groups"),
        P("groups"),
    )
    return jax.shard_map(
        local, mesh=mesh, in_specs=placed, out_specs=P(None, "groups", "ctx"), check_vma=False
    )
```

```python
import functools

import jax
import jax.numpy as jnp
from jax import lax
from jax.experimental import pallas as pl
from jax.experimental.pallas import tpu as pltpu
from jax.sharding import PartitionSpec as P

D = 8192
SINKS = 4


very_low = -1e30
epsilon = 1e-05


def merged_2(shard, axis, combine):
    everything = jax.tree.map(lambda part: lax.all_gather(part, axis), shard)
    first = jax.tree.map(lambda part: part[0], everything)

    def turn(k, so_far):
        return combine(so_far, jax.tree.map(lambda part: part[k], everything))

    return lax.fori_loop(1, lax.axis_size(axis), turn, first)


def combine(earlier, later):
    top_a, total_a, summed_a = earlier
    top_b, total_b, summed_b = later
    highest = jnp.maximum(top_a, top_b)
    factor_a = jnp.exp(top_a - highest)
    factor_b = jnp.exp(top_b - highest)
    return (
        highest,
        total_a * factor_a + total_b * factor_b,
        summed_a * factor_a[..., None] + summed_b * factor_b[..., None],
    )


def arrange(top_val, total_val, summed_val, row_count):
    head_count = top_val.shape[1] * top_val.shape[2]
    top_val = jnp.transpose(top_val, (3, 0, 1, 2)).reshape(row_count, head_count)
    total_val = jnp.transpose(total_val, (3, 0, 1, 2)).reshape(row_count, head_count)
    summed_val = jnp.transpose(summed_val, (3, 0, 1, 2, 4)).reshape(
        row_count, head_count, summed_val.shape[-1]
    )
    return (top_val, total_val, summed_val)


def page_partials(
    query_heads, page_keys, page_values, retrieval, page_table, lengths, window_start, first_page
):
    page_count, page_len, kv_heads, head_dim = page_keys.shape
    batch_size, blocks = page_table.shape
    steps_n = query_heads.shape[0]
    slot_ids = first_page + jnp.arange(page_count, dtype=jnp.int32)
    matches = (page_table[None, :, :] == slot_ids[:, None, None]).astype(jnp.int32)
    owner_req = jnp.sum(
        matches * jnp.arange(batch_size, dtype=jnp.int32)[None, :, None], axis=(1, 2)
    )
    block_ids = jnp.sum(matches * jnp.arange(blocks, dtype=jnp.int32)[None, None, :], axis=(1, 2))
    query_page = query_heads[:, owner_req]
    scores = jnp.einsum(
        "spkgd,ptkd->pkgst", query_page, page_keys, preferred_element_type=jnp.float32
    ) * head_dim ** (-0.5)
    positions = block_ids[:, None] * page_len + jnp.arange(page_len, dtype=jnp.int32)[None, :]
    in_range = positions < lengths[owner_req][:, None]
    recent = (positions < SINKS) | (positions >= window_start[owner_req][:, None])
    visible = in_range[:, None, :] & ((retrieval[None, :, None] == 1) | recent[:, None, :])
    visible = visible[:, :, None, None, :]
    masked = jnp.where(visible, scores, very_low)
    owner_hot = owner_req[:, None] == jnp.arange(batch_size, dtype=jnp.int32)[None, :]
    page_max = jnp.max(masked, axis=-1)
    local_max = jnp.max(
        jnp.where(owner_hot[:, :, None, None, None], page_max[:, None], very_low), axis=0
    )
    row_max = local_max[owner_req]
    weights = jnp.where(visible, jnp.exp(masked - row_max[..., None]), 0.0)
    owner_float = owner_hot.astype(jnp.float32)
    local_total = jnp.einsum(
        "pb,pkgs->bkgs", owner_float, jnp.sum(weights, axis=-1), precision=lax.Precision.HIGHEST
    )
    values = jnp.einsum(
        "pkgst,ptkd->pkgsd",
        weights.astype(jnp.bfloat16),
        page_values,
        preferred_element_type=jnp.float32,
    )
    local_sum = jnp.einsum("pb,pkgsd->bkgsd", owner_float, values, precision=lax.Precision.HIGHEST)
    return arrange(local_max, local_total, local_sum, steps_n * batch_size)


def fresh_partials(query_heads, key_heads, value_heads):
    steps_n, batch_size, kv_heads, group, head_dim = query_heads.shape
    scores = jnp.einsum(
        "sbkgd,ubkd->bkgsu", query_heads, key_heads, preferred_element_type=jnp.float32
    ) * head_dim ** (-0.5)
    causal = jnp.arange(steps_n)[:, None] >= jnp.arange(steps_n)[None, :]
    masked = jnp.where(causal, scores, very_low)
    highest = jnp.max(masked, axis=-1)
    weights = jnp.where(causal, jnp.exp(masked - highest[..., None]), 0.0)
    totals = jnp.sum(weights, axis=-1)
    summed = jnp.einsum(
        "bkgsu,ubkd->bkgsd",
        weights.astype(jnp.bfloat16),
        value_heads,
        preferred_element_type=jnp.float32,
    )
    return arrange(highest, totals, summed, steps_n * batch_size)


def local_small(
    hidden,
    norm_gain,
    w_query,
    w_key,
    w_value,
    w_output,
    key_cache,
    value_cache,
    retrieval,
    page_table,
    lengths,
    window_start,
):
    steps_n, batch_size, width_local = hidden.shape
    row_count = steps_n * batch_size
    page_count, page_len, kv_heads, head_dim = key_cache.shape
    query_width = w_query.shape[1]
    head_count = query_width // head_dim
    floated = hidden.astype(jnp.float32)
    squares = jnp.sum(floated * floated, axis=-1).reshape(row_count, 1)
    normed = (
        (floated * norm_gain.astype(jnp.float32))
        .astype(jnp.bfloat16)
        .reshape(row_count, width_local)
    )
    query_part = jnp.dot(normed, w_query, preferred_element_type=jnp.float32)
    key_part = jnp.dot(normed, w_key, preferred_element_type=jnp.float32)
    value_part = jnp.dot(normed, w_value, preferred_element_type=jnp.float32)
    query_sum, key_sum, value_sum, square_sum = lax.psum(
        (query_part, key_part, value_part, squares), "ctx"
    )
    inv_rms = lax.rsqrt(square_sum / D + epsilon)
    query_heads = (
        (query_sum * inv_rms)
        .astype(jnp.bfloat16)
        .reshape(steps_n, batch_size, kv_heads, head_count // kv_heads, head_dim)
    )
    key_heads = (
        (key_sum * inv_rms).astype(jnp.bfloat16).reshape(steps_n, batch_size, kv_heads, head_dim)
    )
    value_heads = (
        (value_sum * inv_rms).astype(jnp.bfloat16).reshape(steps_n, batch_size, kv_heads, head_dim)
    )
    device = lax.axis_index("ctx")
    local_parts = page_partials(
        query_heads,
        key_cache,
        value_cache,
        retrieval,
        page_table,
        lengths,
        window_start,
        device * page_count,
    )
    fresh_parts = fresh_partials(query_heads, key_heads, value_heads)
    col_share = query_width // lax.axis_size("ctx")
    col_start = device * col_share
    merged = merged_2(local_parts, "ctx", combine)
    highest, totals, summed = combine(merged, fresh_parts)
    attended_full = (
        (summed / totals[..., None]).reshape(row_count, query_width).astype(jnp.bfloat16)
    )
    attended = lax.dynamic_slice_in_dim(attended_full, col_start, col_share, 1)
    partial_out = jnp.dot(attended, w_output, preferred_element_type=jnp.float32)
    reduced = lax.psum_scatter(partial_out, "ctx", scatter_dimension=1, tiled=True)
    return reduced.reshape(steps_n, batch_size, -1).astype(jnp.bfloat16)


def swap_halves(first, second):
    low = lax.broadcasted_iota(jnp.int32, first.shape, 0) < first.shape[0] // 2
    half = first.shape[0] // 2
    return (
        jnp.where(low, first, pltpu.roll(second, half, 0)),
        jnp.where(low, pltpu.roll(first, half, 0), second),
    )


def fused(
    n,
    steps_n,
    batch,
    kv_heads,
    page_len,
    retrieval_ref,
    lengths_ref,
    window_ref,
    hidden_ref,
    gain_ref,
    table_ref,
    wq_hbm,
    wk_hbm,
    wv_hbm,
    wo_hbm,
    keys_hbm,
    values_hbm,
    out_ref,
    wq_v,
    wkv_v,
    wo_v,
    keys_v,
    values_v,
    values_t,
    msg1,
    recv1,
    gath,
    queries,
    queries_t,
    info,
    owners,
    page_max,
    page_total,
    page_sum,
    msg3,
    recv3,
    msg4,
    recv4,
    wq_sem,
    wo_sem,
    wkv_sem,
    keys_sem,
    values_sem,
    send_sem,
    recv_sem,
):
    f32, bf16 = jnp.float32, jnp.bfloat16
    me = lax.axis_index("ctx")
    pages = keys_v.shape[0]
    share = wq_v.shape[2]
    width = share * n
    dim = 128
    width_local = hidden_ref.shape[2]
    scale = dim ** (-0.5)
    half = n // 2

    def peer(i):
        return lax.rem(me + i, n)

    def source(i):
        return lax.rem(me + n - i, n)

    twin = me + 1 - 2 * lax.rem(me, 2)

    def twin_peer(i):
        return lax.rem(twin + i, n)

    def target(k):
        odd = lax.rem(k, 2)
        return lax.rem(me + odd * (twin - me) + k - odd, n)

    def wq_copy(i):
        cols = pl.ds(pl.multiple_of(target(i) * share, 128), share)
        return pltpu.make_async_copy(wq_hbm.at[:, cols], wq_v.at[i], wq_sem.at[i])

    def wo_copy(i):
        cols = pl.ds(pl.multiple_of(target(i) * share, 128), share)
        return pltpu.make_async_copy(wo_hbm.at[:, cols], wo_v.at[i], wo_sem.at[i])

    kv_width = kv_heads * dim
    wk_copy = pltpu.make_async_copy(wk_hbm, wkv_v.at[:, pl.ds(0, kv_width)], wkv_sem.at[0])
    wv_copy = pltpu.make_async_copy(wv_hbm, wkv_v.at[:, pl.ds(kv_width, kv_width)], wkv_sem.at[1])

    def keys_copy(p):
        return pltpu.make_async_copy(keys_hbm.at[p], keys_v.at[p], keys_sem.at[p])

    def values_copy(p):
        return pltpu.make_async_copy(values_hbm.at[p], values_v.at[p], values_sem.at[p])

    def remote(phase, i, from_ref, to_ref, device):
        return pltpu.make_async_remote_copy(
            src_ref=from_ref,
            dst_ref=to_ref,
            send_sem=send_sem.at[phase, i],
            recv_sem=recv_sem.at[phase, i],
            device_id={"ctx": device},
            device_id_type=pl.DeviceIdType.MESH,
        )

    barrier = pltpu.get_barrier_semaphore()

    @pl.loop(1, n)
    def _(i):
        pl.semaphore_signal(
            barrier, inc=1, device_id={"ctx": peer(i)}, device_id_type=pl.DeviceIdType.MESH
        )

    wk_copy.start()
    wv_copy.start()

    @pl.loop(1, half + 1)
    def _(h):
        wq_copy(lax.rem(2 * h, n) + 1).start()

    @pl.loop(1, half + 1)
    def _(h):
        wq_copy(lax.rem(2 * h, n)).start()

    @pl.loop(0, pages)
    def _(p):
        values_copy(p).start()

    @pl.loop(0, pages)
    def _(p):
        keys_copy(p).start()

    @pl.loop(1, half + 1)
    def _(h):
        wo_copy(lax.rem(2 * h, n) + 1).start()

    @pl.loop(1, half + 1)
    def _(h):
        wo_copy(lax.rem(2 * h, n)).start()

    loaded = hidden_ref[...].astype(f32)
    floated = jnp.concatenate(
        [loaded[s, b : b + 1, :] for b in range(batch) for s in range(steps_n)], axis=0
    )
    squares = jnp.sum(floated * floated, axis=1, keepdims=True)
    squares = jnp.broadcast_to(squares, (floated.shape[0], dim))
    normed = (floated * gain_ref[...].astype(f32).reshape(1, width_local)).astype(bf16)

    table = table_ref[...]
    page_id = lax.broadcasted_iota(jnp.int32, (pages, table.shape[1]), 0) + me * pages
    lane_block = lax.broadcasted_iota(jnp.int32, (pages, table.shape[1]), 1).astype(f32)
    owner_of = jnp.zeros((pages, 1), f32)
    base_of = jnp.zeros((pages, 1), f32)
    length_of = jnp.zeros((pages, 1), f32)
    window_of = jnp.zeros((pages, 1), f32)
    for b in range(batch):
        hit = jnp.where(table[b : b + 1, :] == page_id, 1.0, 0.0)
        found = jnp.sum(hit, axis=1, keepdims=True)
        owner_of += found * float(b)
        base_of += jnp.sum(hit * lane_block, axis=1, keepdims=True) * float(page_len)
        length_of += found * lengths_ref[b].astype(f32)
        window_of += found * window_ref[b].astype(f32)
    for row, value in enumerate((owner_of, base_of, length_of, window_of)):
        info[row] = jnp.broadcast_to(value, (pages, dim)).astype(jnp.int32)

    @pl.loop(0, pages)
    def _(p):
        found = jnp.sum(jnp.where(table[1:2, :] == me * pages + p, 1, 0))
        owners[p] = jnp.minimum(found, batch - 1)

    wk_copy.wait()
    wv_copy.wait()
    pl.semaphore_wait(barrier, n - 1)

    def project(i, to_ref):
        wq_copy(i).wait()
        cols = pl.ds(pl.multiple_of(target(i) * dim, 128), dim)
        to_ref[:, pl.ds(0, share)] = jnp.dot(normed, wq_v[i], preferred_element_type=f32)
        to_ref[:, pl.ds(share, dim)] = jnp.dot(normed, wkv_v[:, cols], preferred_element_type=f32)
        to_ref[:, pl.ds(share + dim, dim)] = squares

    def scatter(phase, fill, msg, recv):
        @pl.loop(1, half + 1)
        def _(h):
            e = lax.rem(2 * h, n)
            fill(e + 1, msg.at[e + 1])
            remote(phase, e + 1, msg.at[e + 1], recv.at[peer(e)], twin).start()

        @pl.loop(1, half)
        def _(h):
            e = 2 * h
            fill(e, msg.at[e])
            remote(phase, e + 1, msg.at[e + 1], recv.at[twin_peer(e)], twin).wait_recv()
            msg[e] = msg[e] + recv[twin_peer(e)]
            remote(phase, e, msg.at[e], recv.at[me], peer(e)).start()

        fill(0, msg.at[0])

    scatter(0, project, msg1, recv1)

    @pl.loop(0, pages)
    def _(p):
        values_copy(p).wait()
        values_t[p] = values_v[p].T

    def add_up(phase, msg, recv):
        remote(phase, 1, msg.at[1], recv.at[twin], twin).wait_recv()

        def turn(h, acc):
            e = 2 * h
            remote(phase, e, msg.at[e], recv.at[source(e)], peer(e)).wait_recv()
            return acc + recv[source(e)]

        return lax.fori_loop(1, half, turn, msg[0] + recv[twin])

    summed = add_up(0, msg1, recv1)
    inv_rms = lax.rsqrt(summed[:, share + dim :] / (width_local * n) + epsilon)
    for c in range((share + dim) // dim):
        piece = summed[:, c * dim : (c + 1) * dim] * inv_rms
        gath[me, :, pl.ds(c * dim, dim)] = piece.astype(bf16).astype(f32)

    @pl.loop(1, half)
    def _(h):
        remote(1, 2 * h, gath.at[me], gath.at[me], peer(2 * h)).start()

    remote(1, 1, gath.at[me], gath.at[me], twin).start()

    def spread(j):
        rows = pl.multiple_of(j * 2 * steps_n * batch, 8)
        for c in range(2):
            even = gath[j, :, pl.ds(2 * c * dim, dim)]
            odd = gath[j, :, pl.ds((2 * c + 1) * dim, dim)]
            low, high = swap_halves(even, odd)
            queries[0, pl.ds(rows + 8 * c, 8), :] = low
            queries[1, pl.ds(rows + 8 * c, 8), :] = high

    spread(me)

    @pl.loop(1, half)
    def _(h):
        e = 2 * h
        block = gath.at[source(e)]
        remote(1, e, gath.at[me], block, peer(e)).wait_recv()
        remote(1, e + 1, block, block, twin).start()
        spread(source(e))

    @pl.loop(0, half)
    def _(h):
        e = 2 * h
        origin = lax.rem(twin + n - e, n)
        remote(1, e + 1, gath.at[me], gath.at[origin], twin).wait_recv()
        spread(origin)

    q_rows = queries.shape[1]
    per_head = q_rows // kv_heads
    groups = dim // per_head
    part = page_len // groups
    for b in range(batch):
        turned = queries[b].T
        for i in range(groups):
            queries_t[b, i] = jnp.concatenate(
                [
                    pltpu.roll(turned[:, :dim], per_head * i, 1),
                    pltpu.roll(turned[:, dim:], per_head * i, 1),
                ],
                axis=1,
            ).astype(bf16)

    sub = lax.broadcasted_iota(jnp.int32, (kv_heads, dim), 0)
    lane = lax.broadcasted_iota(jnp.int32, (kv_heads, dim), 1)
    lower = sub < kv_heads // 2
    group = lax.rem(lane // per_head - lax.rem(sub, groups) + groups, groups)
    own_lane = group == 0
    full_head = jnp.zeros((kv_heads, dim), jnp.int32)
    for k in range(kv_heads):
        full_head = jnp.where(sub == k, retrieval_ref[k], full_head)
    full_head = full_head == 1

    own_low, own_high = own_lane & lower, own_lane & ~lower
    token = lax.broadcasted_iota(jnp.int32, (part, kv_heads, dim), 0)

    def page_scores(p):
        query = owners[p]
        merged = None
        for i in range(groups):
            rows = pl.ds(i * part * kv_heads, part * kv_heads)
            scores = jnp.dot(keys_v[p, rows, :], queries_t[query, i], preferred_element_type=f32)
            scores = scores.reshape(part, kv_heads, q_rows)
            scores = jnp.where(lower[None], scores[:, :, :dim], scores[:, :, dim:])
            merged = scores if i == 0 else jnp.where((group == i)[None], scores, merged)
        return merged

    def page_weights(p, merged):
        base = info[1, pl.ds(p, 1), :] + part * group
        until = info[2, pl.ds(p, 1), :] - base
        since = jnp.where(full_head, 0, info[3, pl.ds(p, 1), :]) - base
        sinks = SINKS - base
        visible = (token < until[None]) & ((token >= since[None]) | (token < sinks[None]))
        masked = jnp.where(visible, merged * scale, very_low)
        highest = jnp.max(masked, axis=0)
        for shift in range(groups.bit_length() - 1):
            highest = jnp.maximum(highest, pltpu.roll(highest, per_head << shift, 1))
        weights = jnp.where(visible, jnp.exp(masked - highest[None]), 0.0)
        total = jnp.sum(weights, axis=0)
        for shift in range(groups.bit_length() - 1):
            total = total + pltpu.roll(total, per_head << shift, 1)
        wide = []
        for i in range(groups):
            turned = weights if i == 0 else pltpu.roll(weights, dim - per_head * i, 2)
            both = jnp.concatenate(
                [
                    jnp.where(own_low[None], turned, 0.0),
                    jnp.where(own_high[None], turned, 0.0),
                ],
                axis=2,
            )
            wide.append(both.reshape(part * kv_heads, q_rows).astype(bf16))
        return highest, total, jnp.concatenate(wide, axis=0)

    at_once = 4

    @pl.loop(0, pages)
    def _(p):
        keys_copy(p).wait()

    @pl.loop(0, pages // at_once)
    def _(g):
        block = [g * at_once + u for u in range(at_once)]
        scored = [page_scores(p) for p in block]
        weighed = [page_weights(p, merged) for p, merged in zip(block, scored)]
        summed = [
            jnp.dot(values_t[p], wide, preferred_element_type=f32)
            for p, (_, _, wide) in zip(block, weighed)
        ]
        for p, (highest, total, _), page in zip(block, weighed, summed):
            page_max[p] = highest
            page_total[p] = total
            page_sum[p] = page

    def lanes_of(stat):
        kept = jnp.where(own_lane, stat, 0.0)
        return jnp.concatenate(
            [
                jnp.sum(jnp.where(lower, kept, 0.0), axis=0, keepdims=True),
                jnp.sum(jnp.where(lower, 0.0, kept), axis=0, keepdims=True),
            ],
            axis=1,
        )

    def top_turn(p, tops):
        owner = info[0, pl.ds(p, 1), :]
        return tuple(
            jnp.where(owner == b, jnp.maximum(top, page_max[p]), top) for b, top in enumerate(tops)
        )

    start = jnp.full((kv_heads, dim), very_low, f32)
    tops = lax.fori_loop(0, pages, top_turn, (start,) * batch)

    def sum_turn(p, totals):
        owner = info[0, pl.ds(p, 1), :]
        top = jnp.where(owner == 1, tops[1], tops[0])
        factor = jnp.exp(page_max[p] - top)
        term = factor * page_total[p]
        totals = tuple(total + jnp.where(owner == b, term, 0.0) for b, total in enumerate(totals))
        page_sum[p] = page_sum[p] * lanes_of(factor)
        return totals

    totals = lax.fori_loop(0, pages, sum_turn, (jnp.zeros((kv_heads, dim), f32),) * batch)

    for b in range(batch):
        acc = jnp.zeros((dim, q_rows), f32)
        for p in range(pages):
            owner = info[0, pl.ds(p, 1), :]
            wide_owner = jnp.concatenate([owner, owner], axis=1)
            acc += jnp.where(wide_owner == b, page_sum[p], 0.0)
        msg3[:, pl.ds(16 * b, 16), :] = acc.T.reshape(n, q_rows // n, dim)
    stats = jnp.concatenate(
        [lanes_of(tops[0]), lanes_of(tops[1]), lanes_of(totals[0]), lanes_of(totals[1])]
        + [jnp.zeros((4, q_rows), f32)],
        axis=0,
    )
    span = q_rows // n
    for j in range(n):
        at = j * span // dim * dim
        moved = (dim - (j * span - at)) % dim
        piece = stats[:, at : at + dim]
        msg3[j, pl.ds(32, 8), :] = piece if moved == 0 else pltpu.roll(piece, moved, 1)

    @pl.loop(1, n)
    def _(i):
        remote(2, i, msg3.at[peer(i)], recv3.at[me], peer(i)).start()

    recv3[me] = msg3[me]

    mine = pl.ds(pl.multiple_of(me * 16, 8), 16)
    head = me // 2
    new_key = gath[head, :, pl.ds(share, dim)]
    new_value = gath[kv_heads + head, :, pl.ds(share, dim)]
    row = lax.broadcasted_iota(jnp.int32, (8, dim), 0)
    col = lax.broadcasted_iota(jnp.int32, (8, dim), 1)
    fresh_max = jnp.full((8, dim), very_low, f32)
    fresh_total = jnp.zeros((8, dim), f32)
    fresh_sum = []
    for b in range(batch):
        own_query = jnp.concatenate([queries[b, mine, :]] * (dim // 16), axis=0)
        fresh = lax.dot_general(
            new_key, own_query, (((1,), (1,)), ((), ())), preferred_element_type=f32
        )
        causal = (row // steps_n == b) & (lax.rem(row, steps_n) <= lax.rem(col, steps_n))
        fresh = jnp.where(causal, fresh * scale, very_low)
        highest = jnp.max(fresh, axis=0, keepdims=True)
        weights = jnp.where(causal, jnp.exp(fresh - highest), 0.0)
        fresh_max = jnp.where(row == b, highest, fresh_max)
        fresh_total = jnp.where(row == b, jnp.sum(weights, axis=0, keepdims=True), fresh_total)
        fresh_sum.append(
            lax.dot_general(
                weights.astype(bf16).astype(f32),
                new_value,
                (((0,), (0,)), ((), ())),
                preferred_element_type=f32,
            )[:16]
        )

    @pl.loop(1, n)
    def _(i):
        remote(2, i, msg3.at[peer(i)], recv3.at[source(i)], peer(i)).wait_recv()

    parts = recv3[:, pl.ds(32, 8), :]
    top = jnp.maximum(jnp.max(parts, axis=0), fresh_max)
    factor = jnp.exp(parts - top[None])
    fresh_factor = jnp.exp(fresh_max - top)
    total = jnp.sum(factor * pltpu.roll(parts, 8 - batch, 1), axis=0) + fresh_factor * fresh_total
    total = jnp.where(row < batch, total, 1.0)
    factor = factor / total[None]
    fresh_factor = pltpu.roll(fresh_factor / total, 4, 0)
    factor = jnp.where((row < 4)[None], factor, fresh_factor[None]).reshape(n * 8, dim).T[:16]
    attended = []
    for b in range(batch):
        acc = fresh_sum[b] * factor[:, 4 + b : 5 + b]
        for j in range(n):
            acc += recv3[j, pl.ds(16 * b, 16), :] * factor[:, 8 * j + b : 8 * j + b + 1]
        attended.append(acc)
    first = swap_halves(attended[0][:8], attended[1][:8])
    second = swap_halves(attended[0][8:], attended[1][8:])
    attended = jnp.concatenate(first + second, axis=1).astype(bf16)

    def project_out(i, to_ref):
        wo_copy(i).wait()
        to_ref[...] = jnp.dot(attended, wo_v[i], preferred_element_type=f32)

    scatter(3, project_out, msg4, recv4)
    result = add_up(3, msg4, recv4)
    for s in range(steps_n):
        out_ref[s] = jnp.concatenate(
            [result[b * steps_n + s : b * steps_n + s + 1] for b in range(batch)], axis=0
        ).astype(out_ref.dtype)

    @pl.loop(1, n)
    def _(i):
        remote(0, i, msg1.at[i], recv1.at[me], peer(i)).wait_send()
        remote(1, i, gath.at[me], gath.at[me], peer(i)).wait_send()
        remote(2, i, msg3.at[peer(i)], recv3.at[me], peer(i)).wait_send()
        remote(3, i, msg4.at[i], recv4.at[me], peer(i)).wait_send()


def local(
    hidden,
    norm_gain,
    w_query,
    w_key,
    w_value,
    w_output,
    key_cache,
    value_cache,
    retrieval,
    page_table,
    lengths,
    window_start,
):
    n = lax.axis_size("ctx")
    steps_n, batch, width_local = hidden.shape
    pages, page_len, kv_heads, dim = key_cache.shape
    query_width = w_query.shape[1]
    share = query_width // n
    rows = steps_n * batch
    q_rows = query_width // dim * steps_n
    if pages % 4 or (n, share, rows, batch, kv_heads, dim) != (2 * kv_heads, 4 * dim, 8, 2, 8, 128):
        return local_small(
            hidden,
            norm_gain,
            w_query,
            w_key,
            w_value,
            w_output,
            key_cache,
            value_cache,
            retrieval,
            page_table,
            lengths,
            window_start,
        )
    f32, bf16 = jnp.float32, jnp.bfloat16
    smem = pl.BlockSpec(memory_space=pltpu.SMEM)
    vmem = pl.BlockSpec(memory_space=pltpu.VMEM)
    hbm = pl.BlockSpec(memory_space=pl.ANY)
    dma = pltpu.SemaphoreType.DMA
    out = pl.pallas_call(
        functools.partial(fused, n, steps_n, batch, kv_heads, page_len),
        out_shape=jax.ShapeDtypeStruct((steps_n, batch, w_output.shape[1] // n), bf16),
        in_specs=[smem] * 3 + [vmem] * 3 + [hbm] * 6,
        out_specs=vmem,
        scratch_shapes=[
            pltpu.VMEM((n, width_local, share), bf16),
            pltpu.VMEM((width_local, 2 * kv_heads * dim), bf16),
            pltpu.VMEM((n, share, w_output.shape[1] // n), bf16),
            pltpu.VMEM((pages, page_len * kv_heads, dim), bf16),
            pltpu.VMEM((pages, page_len * kv_heads, dim), bf16),
            pltpu.VMEM((pages, dim, page_len * kv_heads), bf16),
            pltpu.VMEM((n, rows, share + 2 * dim), f32),
            pltpu.VMEM((n, rows, share + 2 * dim), f32),
            pltpu.VMEM((n, rows, share + dim), f32),
            pltpu.VMEM((batch, q_rows, dim), f32),
            pltpu.VMEM((batch, dim // (q_rows // kv_heads), dim, q_rows), bf16),
            pltpu.VMEM((4, pages, dim), jnp.int32),
            pltpu.SMEM((pages,), jnp.int32),
            pltpu.VMEM((pages, kv_heads, dim), f32),
            pltpu.VMEM((pages, kv_heads, dim), f32),
            pltpu.VMEM((pages, dim, q_rows), f32),
            pltpu.VMEM((n, 40, dim), f32),
            pltpu.VMEM((n, 40, dim), f32),
            pltpu.VMEM((n, rows, share), f32),
            pltpu.VMEM((n, rows, share), f32),
            dma((n,)),
            dma((n,)),
            dma((2,)),
            dma((pages,)),
            dma((pages,)),
            dma((4, n)),
            dma((4, n)),
        ],
        compiler_params=pltpu.CompilerParams(
            collective_id=0, has_side_effects=True, vmem_limit_bytes=56 * 2**20
        ),
    )(
        retrieval,
        lengths,
        window_start,
        hidden,
        norm_gain,
        page_table,
        w_query,
        w_key,
        w_value,
        w_output,
        key_cache.reshape(pages, page_len * kv_heads, dim),
        value_cache.reshape(pages, page_len * kv_heads, dim),
    )
    return out


def solution(mesh):
    placed = (
        P(None, "groups", "ctx"),
        P("ctx"),
        P("ctx", None),
        P("ctx", None),
        P("ctx", None),
        P("ctx", None),
        P(("groups", "ctx"), None, None, None),
        P(("groups", "ctx"), None, None, None),
        P(),
        P("groups", None),
        P("groups"),
        P("groups"),
    )
    return jax.shard_map(
        local, mesh=mesh, in_specs=placed, out_specs=P(None, "groups", "ctx"), check_vma=False
    )
```

```python
import functools

import jax
import jax.numpy as jnp
from jax import lax
from jax.experimental import pallas as pl
from jax.experimental.pallas import tpu as pltpu
from jax.sharding import PartitionSpec as P

D = 8192
SINKS = 4


very_low = -1e30
epsilon = 1e-05


def merged_2(shard, axis, combine):
    everything = jax.tree.map(lambda part: lax.all_gather(part, axis), shard)
    first = jax.tree.map(lambda part: part[0], everything)

    def turn(k, so_far):
        return combine(so_far, jax.tree.map(lambda part: part[k], everything))

    return lax.fori_loop(1, lax.axis_size(axis), turn, first)


def combine(earlier, later):
    top_a, total_a, summed_a = earlier
    top_b, total_b, summed_b = later
    highest = jnp.maximum(top_a, top_b)
    factor_a = jnp.exp(top_a - highest)
    factor_b = jnp.exp(top_b - highest)
    return (
        highest,
        total_a * factor_a + total_b * factor_b,
        summed_a * factor_a[..., None] + summed_b * factor_b[..., None],
    )


def arrange(top_val, total_val, summed_val, row_count):
    head_count = top_val.shape[1] * top_val.shape[2]
    top_val = jnp.transpose(top_val, (3, 0, 1, 2)).reshape(row_count, head_count)
    total_val = jnp.transpose(total_val, (3, 0, 1, 2)).reshape(row_count, head_count)
    summed_val = jnp.transpose(summed_val, (3, 0, 1, 2, 4)).reshape(
        row_count, head_count, summed_val.shape[-1]
    )
    return (top_val, total_val, summed_val)


def page_partials(
    query_heads, page_keys, page_values, retrieval, page_table, lengths, window_start, first_page
):
    page_count, page_len, kv_heads, head_dim = page_keys.shape
    batch_size, blocks = page_table.shape
    steps_n = query_heads.shape[0]
    slot_ids = first_page + jnp.arange(page_count, dtype=jnp.int32)
    matches = (page_table[None, :, :] == slot_ids[:, None, None]).astype(jnp.int32)
    owner_req = jnp.sum(
        matches * jnp.arange(batch_size, dtype=jnp.int32)[None, :, None], axis=(1, 2)
    )
    block_ids = jnp.sum(matches * jnp.arange(blocks, dtype=jnp.int32)[None, None, :], axis=(1, 2))
    query_page = query_heads[:, owner_req]
    scores = jnp.einsum(
        "spkgd,ptkd->pkgst", query_page, page_keys, preferred_element_type=jnp.float32
    ) * head_dim ** (-0.5)
    positions = block_ids[:, None] * page_len + jnp.arange(page_len, dtype=jnp.int32)[None, :]
    in_range = positions < lengths[owner_req][:, None]
    recent = (positions < SINKS) | (positions >= window_start[owner_req][:, None])
    visible = in_range[:, None, :] & ((retrieval[None, :, None] == 1) | recent[:, None, :])
    visible = visible[:, :, None, None, :]
    masked = jnp.where(visible, scores, very_low)
    owner_hot = owner_req[:, None] == jnp.arange(batch_size, dtype=jnp.int32)[None, :]
    page_max = jnp.max(masked, axis=-1)
    local_max = jnp.max(
        jnp.where(owner_hot[:, :, None, None, None], page_max[:, None], very_low), axis=0
    )
    row_max = local_max[owner_req]
    weights = jnp.where(visible, jnp.exp(masked - row_max[..., None]), 0.0)
    owner_float = owner_hot.astype(jnp.float32)
    local_total = jnp.einsum(
        "pb,pkgs->bkgs", owner_float, jnp.sum(weights, axis=-1), precision=lax.Precision.HIGHEST
    )
    values = jnp.einsum(
        "pkgst,ptkd->pkgsd",
        weights.astype(jnp.bfloat16),
        page_values,
        preferred_element_type=jnp.float32,
    )
    local_sum = jnp.einsum("pb,pkgsd->bkgsd", owner_float, values, precision=lax.Precision.HIGHEST)
    return arrange(local_max, local_total, local_sum, steps_n * batch_size)


def fresh_partials(query_heads, key_heads, value_heads):
    steps_n, batch_size, kv_heads, group, head_dim = query_heads.shape
    scores = jnp.einsum(
        "sbkgd,ubkd->bkgsu", query_heads, key_heads, preferred_element_type=jnp.float32
    ) * head_dim ** (-0.5)
    causal = jnp.arange(steps_n)[:, None] >= jnp.arange(steps_n)[None, :]
    masked = jnp.where(causal, scores, very_low)
    highest = jnp.max(masked, axis=-1)
    weights = jnp.where(causal, jnp.exp(masked - highest[..., None]), 0.0)
    totals = jnp.sum(weights, axis=-1)
    summed = jnp.einsum(
        "bkgsu,ubkd->bkgsd",
        weights.astype(jnp.bfloat16),
        value_heads,
        preferred_element_type=jnp.float32,
    )
    return arrange(highest, totals, summed, steps_n * batch_size)


def local_small(
    hidden,
    norm_gain,
    w_query,
    w_key,
    w_value,
    w_output,
    key_cache,
    value_cache,
    retrieval,
    page_table,
    lengths,
    window_start,
):
    steps_n, batch_size, width_local = hidden.shape
    row_count = steps_n * batch_size
    page_count, page_len, kv_heads, head_dim = key_cache.shape
    query_width = w_query.shape[1]
    head_count = query_width // head_dim
    floated = hidden.astype(jnp.float32)
    squares = jnp.sum(floated * floated, axis=-1).reshape(row_count, 1)
    normed = (
        (floated * norm_gain.astype(jnp.float32))
        .astype(jnp.bfloat16)
        .reshape(row_count, width_local)
    )
    query_part = jnp.dot(normed, w_query, preferred_element_type=jnp.float32)
    key_part = jnp.dot(normed, w_key, preferred_element_type=jnp.float32)
    value_part = jnp.dot(normed, w_value, preferred_element_type=jnp.float32)
    query_sum, key_sum, value_sum, square_sum = lax.psum(
        (query_part, key_part, value_part, squares), "ctx"
    )
    inv_rms = lax.rsqrt(square_sum / D + epsilon)
    query_heads = (
        (query_sum * inv_rms)
        .astype(jnp.bfloat16)
        .reshape(steps_n, batch_size, kv_heads, head_count // kv_heads, head_dim)
    )
    key_heads = (
        (key_sum * inv_rms).astype(jnp.bfloat16).reshape(steps_n, batch_size, kv_heads, head_dim)
    )
    value_heads = (
        (value_sum * inv_rms).astype(jnp.bfloat16).reshape(steps_n, batch_size, kv_heads, head_dim)
    )
    device = lax.axis_index("ctx")
    local_parts = page_partials(
        query_heads,
        key_cache,
        value_cache,
        retrieval,
        page_table,
        lengths,
        window_start,
        device * page_count,
    )
    fresh_parts = fresh_partials(query_heads, key_heads, value_heads)
    col_share = query_width // lax.axis_size("ctx")
    col_start = device * col_share
    merged = merged_2(local_parts, "ctx", combine)
    highest, totals, summed = combine(merged, fresh_parts)
    attended_full = (
        (summed / totals[..., None]).reshape(row_count, query_width).astype(jnp.bfloat16)
    )
    attended = lax.dynamic_slice_in_dim(attended_full, col_start, col_share, 1)
    partial_out = jnp.dot(attended, w_output, preferred_element_type=jnp.float32)
    reduced = lax.psum_scatter(partial_out, "ctx", scatter_dimension=1, tiled=True)
    return reduced.reshape(steps_n, batch_size, -1).astype(jnp.bfloat16)


def swap_halves(first, second):
    low = lax.broadcasted_iota(jnp.int32, first.shape, 0) < first.shape[0] // 2
    half = first.shape[0] // 2
    return (
        jnp.where(low, first, pltpu.roll(second, half, 0)),
        jnp.where(low, pltpu.roll(first, half, 0), second),
    )


def fused(
    n,
    steps_n,
    batch,
    kv_heads,
    page_len,
    retrieval_ref,
    lengths_ref,
    window_ref,
    hidden_ref,
    gain_ref,
    table_ref,
    wq_hbm,
    wk_hbm,
    wv_hbm,
    wo_hbm,
    keys_hbm,
    values_hbm,
    out_ref,
    wq_v,
    wkv_v,
    wo_v,
    keys_v,
    values_v,
    values_t,
    msg1,
    recv1,
    gath,
    queries,
    queries_t,
    info,
    owners,
    page_max,
    page_total,
    page_sum,
    msg3,
    recv3,
    msg4,
    recv4,
    wq_sem,
    wo_sem,
    wkv_sem,
    keys_sem,
    values_sem,
    send_sem,
    recv_sem,
):
    f32, bf16 = jnp.float32, jnp.bfloat16
    me = lax.axis_index("ctx")
    pages = keys_v.shape[0]
    share = wq_v.shape[2]
    width = share * n
    dim = 128
    width_local = hidden_ref.shape[2]
    scale = dim ** (-0.5)
    half = n // 2

    def peer(i):
        return lax.rem(me + i, n)

    def source(i):
        return lax.rem(me + n - i, n)

    twin = me + 1 - 2 * lax.rem(me, 2)

    def twin_peer(i):
        return lax.rem(twin + i, n)

    def target(k):
        odd = lax.rem(k, 2)
        return lax.rem(me + odd * (twin - me) + k - odd, n)

    def wq_copy(i):
        cols = pl.ds(pl.multiple_of(target(i) * share, 128), share)
        return pltpu.make_async_copy(wq_hbm.at[:, cols], wq_v.at[i], wq_sem.at[i])

    def wo_copy(i):
        cols = pl.ds(pl.multiple_of(target(i) * share, 128), share)
        return pltpu.make_async_copy(wo_hbm.at[:, cols], wo_v.at[i], wo_sem.at[i])

    kv_width = kv_heads * dim
    wk_copy = pltpu.make_async_copy(wk_hbm, wkv_v.at[:, pl.ds(0, kv_width)], wkv_sem.at[0])
    wv_copy = pltpu.make_async_copy(wv_hbm, wkv_v.at[:, pl.ds(kv_width, kv_width)], wkv_sem.at[1])

    def keys_copy(p):
        return pltpu.make_async_copy(keys_hbm.at[p], keys_v.at[p], keys_sem.at[p])

    def values_copy(p):
        return pltpu.make_async_copy(values_hbm.at[p], values_v.at[p], values_sem.at[p])

    def remote(phase, i, from_ref, to_ref, device):
        return pltpu.make_async_remote_copy(
            src_ref=from_ref,
            dst_ref=to_ref,
            send_sem=send_sem.at[phase, i],
            recv_sem=recv_sem.at[phase, i],
            device_id={"ctx": device},
            device_id_type=pl.DeviceIdType.MESH,
        )

    barrier = pltpu.get_barrier_semaphore()

    @pl.loop(1, n)
    def _(i):
        pl.semaphore_signal(
            barrier, inc=1, device_id={"ctx": peer(i)}, device_id_type=pl.DeviceIdType.MESH
        )

    wk_copy.start()
    wv_copy.start()

    @pl.loop(1, half + 1)
    def _(h):
        wq_copy(lax.rem(2 * h, n) + 1).start()

    @pl.loop(1, half + 1)
    def _(h):
        wq_copy(lax.rem(2 * h, n)).start()

    @pl.loop(0, pages)
    def _(p):
        values_copy(p).start()

    @pl.loop(0, pages)
    def _(p):
        keys_copy(p).start()

    @pl.loop(1, half + 1)
    def _(h):
        wo_copy(lax.rem(2 * h, n) + 1).start()

    @pl.loop(1, half + 1)
    def _(h):
        wo_copy(lax.rem(2 * h, n)).start()

    loaded = hidden_ref[...].astype(f32)
    floated = jnp.concatenate(
        [loaded[s, b : b + 1, :] for b in range(batch) for s in range(steps_n)], axis=0
    )
    squares = jnp.sum(floated * floated, axis=1, keepdims=True)
    squares = jnp.broadcast_to(squares, (floated.shape[0], dim))
    normed = (floated * gain_ref[...].astype(f32).reshape(1, width_local)).astype(bf16)

    table = table_ref[...]
    page_id = lax.broadcasted_iota(jnp.int32, (pages, table.shape[1]), 0) + me * pages
    lane_block = lax.broadcasted_iota(jnp.int32, (pages, table.shape[1]), 1).astype(f32)
    owner_of = jnp.zeros((pages, 1), f32)
    base_of = jnp.zeros((pages, 1), f32)
    length_of = jnp.zeros((pages, 1), f32)
    window_of = jnp.zeros((pages, 1), f32)
    for b in range(batch):
        hit = jnp.where(table[b : b + 1, :] == page_id, 1.0, 0.0)
        found = jnp.sum(hit, axis=1, keepdims=True)
        owner_of += found * float(b)
        base_of += jnp.sum(hit * lane_block, axis=1, keepdims=True) * float(page_len)
        length_of += found * lengths_ref[b].astype(f32)
        window_of += found * window_ref[b].astype(f32)
    for row, value in enumerate((owner_of, base_of, length_of, window_of)):
        info[row] = jnp.broadcast_to(value, (pages, dim)).astype(jnp.int32)

    @pl.loop(0, pages)
    def _(p):
        found = jnp.sum(jnp.where(table[1:2, :] == me * pages + p, 1, 0))
        owners[p] = jnp.minimum(found, batch - 1)

    wk_copy.wait()
    wv_copy.wait()
    pl.semaphore_wait(barrier, n - 1)

    def project(i, to_ref):
        wq_copy(i).wait()
        cols = pl.ds(pl.multiple_of(target(i) * dim, 128), dim)
        to_ref[:, pl.ds(0, share)] = jnp.dot(normed, wq_v[i], preferred_element_type=f32)
        to_ref[:, pl.ds(share, dim)] = jnp.dot(normed, wkv_v[:, cols], preferred_element_type=f32)
        to_ref[:, pl.ds(share + dim, dim)] = squares

    def scatter(phase, fill, msg, recv):
        @pl.loop(1, half + 1)
        def _(h):
            e = lax.rem(2 * h, n)
            fill(e + 1, msg.at[e + 1])
            remote(phase, e + 1, msg.at[e + 1], recv.at[peer(e)], twin).start()

        @pl.loop(1, half)
        def _(h):
            e = 2 * h
            fill(e, msg.at[e])
            remote(phase, e + 1, msg.at[e + 1], recv.at[twin_peer(e)], twin).wait_recv()
            msg[e] = msg[e] + recv[twin_peer(e)]
            remote(phase, e, msg.at[e], recv.at[me], peer(e)).start()

        fill(0, msg.at[0])

    scatter(0, project, msg1, recv1)

    @pl.loop(0, pages)
    def _(p):
        values_copy(p).wait()
        values_t[p] = values_v[p].T

    def add_up(phase, msg, recv):
        remote(phase, 1, msg.at[1], recv.at[twin], twin).wait_recv()

        def turn(h, acc):
            e = 2 * h
            remote(phase, e, msg.at[e], recv.at[source(e)], peer(e)).wait_recv()
            return acc + recv[source(e)]

        return lax.fori_loop(1, half, turn, msg[0] + recv[twin])

    summed = add_up(0, msg1, recv1)
    inv_rms = lax.rsqrt(summed[:, share + dim :] / (width_local * n) + epsilon)
    for c in range((share + dim) // dim):
        piece = summed[:, c * dim : (c + 1) * dim] * inv_rms
        gath[me, :, pl.ds(c * dim, dim)] = piece.astype(bf16).astype(f32)

    @pl.loop(1, half)
    def _(h):
        remote(1, 2 * h, gath.at[me], gath.at[me], peer(2 * h)).start()

    remote(1, 1, gath.at[me], gath.at[me], twin).start()

    def spread(j):
        rows = pl.multiple_of(j * 2 * steps_n * batch, 8)
        for c in range(2):
            even = gath[j, :, pl.ds(2 * c * dim, dim)]
            odd = gath[j, :, pl.ds((2 * c + 1) * dim, dim)]
            low, high = swap_halves(even, odd)
            queries[0, pl.ds(rows + 8 * c, 8), :] = low
            queries[1, pl.ds(rows + 8 * c, 8), :] = high

    spread(me)

    @pl.loop(1, half)
    def _(h):
        e = 2 * h
        block = gath.at[source(e)]
        remote(1, e, gath.at[me], block, peer(e)).wait_recv()
        remote(1, e + 1, block, block, twin).start()
        spread(source(e))

    @pl.loop(0, half)
    def _(h):
        e = 2 * h
        origin = lax.rem(twin + n - e, n)
        remote(1, e + 1, gath.at[me], gath.at[origin], twin).wait_recv()
        spread(origin)

    q_rows = queries.shape[1]
    per_head = q_rows // kv_heads
    groups = dim // per_head
    part = page_len // groups
    for b in range(batch):
        turned = queries[b].T
        for i in range(groups):
            queries_t[b, i] = jnp.concatenate(
                [
                    pltpu.roll(turned[:, :dim], per_head * i, 1),
                    pltpu.roll(turned[:, dim:], per_head * i, 1),
                ],
                axis=1,
            ).astype(bf16)

    sub = lax.broadcasted_iota(jnp.int32, (kv_heads, dim), 0)
    lane = lax.broadcasted_iota(jnp.int32, (kv_heads, dim), 1)
    lower = sub < kv_heads // 2
    group = lax.rem(lane // per_head - lax.rem(sub, groups) + groups, groups)
    own_lane = group == 0
    full_head = jnp.zeros((kv_heads, dim), jnp.int32)
    for k in range(kv_heads):
        full_head = jnp.where(sub == k, retrieval_ref[k], full_head)
    full_head = full_head == 1

    own_low, own_high = own_lane & lower, own_lane & ~lower
    token = lax.broadcasted_iota(jnp.int32, (part, kv_heads, dim), 0)

    def page_scores(p):
        query = owners[p]
        merged = None
        for i in range(groups):
            rows = pl.ds(i * part * kv_heads, part * kv_heads)
            scores = jnp.dot(keys_v[p, rows, :], queries_t[query, i], preferred_element_type=f32)
            scores = scores.reshape(part, kv_heads, q_rows)
            scores = jnp.where(lower[None], scores[:, :, :dim], scores[:, :, dim:])
            merged = scores if i == 0 else jnp.where((group == i)[None], scores, merged)
        return merged

    def page_weights(p, merged):
        base = info[1, pl.ds(p, 1), :] + part * group
        until = info[2, pl.ds(p, 1), :] - base
        since = jnp.where(full_head, 0, info[3, pl.ds(p, 1), :]) - base
        sinks = SINKS - base
        visible = (token < until[None]) & ((token >= since[None]) | (token < sinks[None]))
        masked = jnp.where(visible, merged * scale, very_low)
        highest = jnp.max(masked, axis=0)
        for shift in range(groups.bit_length() - 1):
            highest = jnp.maximum(highest, pltpu.roll(highest, per_head << shift, 1))
        weights = jnp.where(visible, jnp.exp(masked - highest[None]), 0.0)
        total = jnp.sum(weights, axis=0)
        for shift in range(groups.bit_length() - 1):
            total = total + pltpu.roll(total, per_head << shift, 1)
        wide = []
        for i in range(groups):
            turned = weights if i == 0 else pltpu.roll(weights, dim - per_head * i, 2)
            both = jnp.concatenate(
                [
                    jnp.where(own_low[None], turned, 0.0),
                    jnp.where(own_high[None], turned, 0.0),
                ],
                axis=2,
            )
            wide.append(both.reshape(part * kv_heads, q_rows).astype(bf16))
        return highest, total, jnp.concatenate(wide, axis=0)

    at_once = 8

    @pl.loop(0, pages)
    def _(p):
        keys_copy(p).wait()

    @pl.loop(0, pages // at_once)
    def _(g):
        block = [g * at_once + u for u in range(at_once)]
        scored = [page_scores(p) for p in block]
        weighed = [page_weights(p, merged) for p, merged in zip(block, scored)]
        summed = [
            jnp.dot(values_t[p], wide, preferred_element_type=f32)
            for p, (_, _, wide) in zip(block, weighed)
        ]
        for p, (highest, total, _), page in zip(block, weighed, summed):
            page_max[p] = highest
            page_total[p] = total
            page_sum[p] = page

    def lanes_of(stat):
        kept = jnp.where(own_lane, stat, 0.0)
        return jnp.concatenate(
            [
                jnp.sum(jnp.where(lower, kept, 0.0), axis=0, keepdims=True),
                jnp.sum(jnp.where(lower, 0.0, kept), axis=0, keepdims=True),
            ],
            axis=1,
        )

    def top_turn(p, tops):
        owner = info[0, pl.ds(p, 1), :]
        return tuple(
            jnp.where(owner == b, jnp.maximum(top, page_max[p]), top) for b, top in enumerate(tops)
        )

    start = jnp.full((kv_heads, dim), very_low, f32)
    tops = lax.fori_loop(0, pages, top_turn, (start,) * batch)

    def sum_turn(p, totals):
        owner = info[0, pl.ds(p, 1), :]
        top = jnp.where(owner == 1, tops[1], tops[0])
        factor = jnp.exp(page_max[p] - top)
        term = factor * page_total[p]
        totals = tuple(total + jnp.where(owner == b, term, 0.0) for b, total in enumerate(totals))
        page_sum[p] = page_sum[p] * lanes_of(factor)
        return totals

    totals = lax.fori_loop(0, pages, sum_turn, (jnp.zeros((kv_heads, dim), f32),) * batch)

    for b in range(batch):
        acc = jnp.zeros((dim, q_rows), f32)
        for p in range(pages):
            owner = info[0, pl.ds(p, 1), :]
            wide_owner = jnp.concatenate([owner, owner], axis=1)
            acc += jnp.where(wide_owner == b, page_sum[p], 0.0)
        msg3[:, pl.ds(16 * b, 16), :] = acc.T.reshape(n, q_rows // n, dim)
    stats = jnp.concatenate(
        [lanes_of(tops[0]), lanes_of(tops[1]), lanes_of(totals[0]), lanes_of(totals[1])]
        + [jnp.zeros((4, q_rows), f32)],
        axis=0,
    )
    span = q_rows // n
    for j in range(n):
        at = j * span // dim * dim
        moved = (dim - (j * span - at)) % dim
        piece = stats[:, at : at + dim]
        msg3[j, pl.ds(32, 8), :] = piece if moved == 0 else pltpu.roll(piece, moved, 1)

    @pl.loop(1, n)
    def _(i):
        remote(2, i, msg3.at[peer(i)], recv3.at[me], peer(i)).start()

    recv3[me] = msg3[me]

    mine = pl.ds(pl.multiple_of(me * 16, 8), 16)
    head = me // 2
    new_key = gath[head, :, pl.ds(share, dim)]
    new_value = gath[kv_heads + head, :, pl.ds(share, dim)]
    row = lax.broadcasted_iota(jnp.int32, (8, dim), 0)
    col = lax.broadcasted_iota(jnp.int32, (8, dim), 1)
    fresh_max = jnp.full((8, dim), very_low, f32)
    fresh_total = jnp.zeros((8, dim), f32)
    fresh_sum = []
    for b in range(batch):
        own_query = jnp.concatenate([queries[b, mine, :]] * (dim // 16), axis=0)
        fresh = lax.dot_general(
            new_key, own_query, (((1,), (1,)), ((), ())), preferred_element_type=f32
        )
        causal = (row // steps_n == b) & (lax.rem(row, steps_n) <= lax.rem(col, steps_n))
        fresh = jnp.where(causal, fresh * scale, very_low)
        highest = jnp.max(fresh, axis=0, keepdims=True)
        weights = jnp.where(causal, jnp.exp(fresh - highest), 0.0)
        fresh_max = jnp.where(row == b, highest, fresh_max)
        fresh_total = jnp.where(row == b, jnp.sum(weights, axis=0, keepdims=True), fresh_total)
        fresh_sum.append(
            lax.dot_general(
                weights.astype(bf16).astype(f32),
                new_value,
                (((0,), (0,)), ((), ())),
                preferred_element_type=f32,
            )[:16]
        )

    @pl.loop(1, n)
    def _(i):
        remote(2, i, msg3.at[peer(i)], recv3.at[source(i)], peer(i)).wait_recv()

    parts = recv3[:, pl.ds(32, 8), :]
    top = jnp.maximum(jnp.max(parts, axis=0), fresh_max)
    factor = jnp.exp(parts - top[None])
    fresh_factor = jnp.exp(fresh_max - top)
    total = jnp.sum(factor * pltpu.roll(parts, 8 - batch, 1), axis=0) + fresh_factor * fresh_total
    total = jnp.where(row < batch, total, 1.0)
    factor = factor / total[None]
    fresh_factor = pltpu.roll(fresh_factor / total, 4, 0)
    factor = jnp.where((row < 4)[None], factor, fresh_factor[None]).reshape(n * 8, dim).T[:16]
    attended = []
    for b in range(batch):
        acc = fresh_sum[b] * factor[:, 4 + b : 5 + b]
        for j in range(n):
            acc += recv3[j, pl.ds(16 * b, 16), :] * factor[:, 8 * j + b : 8 * j + b + 1]
        attended.append(acc)
    first = swap_halves(attended[0][:8], attended[1][:8])
    second = swap_halves(attended[0][8:], attended[1][8:])
    attended = jnp.concatenate(first + second, axis=1).astype(bf16)

    def project_out(i, to_ref):
        wo_copy(i).wait()
        to_ref[...] = jnp.dot(attended, wo_v[i], preferred_element_type=f32)

    scatter(3, project_out, msg4, recv4)
    result = add_up(3, msg4, recv4)
    for s in range(steps_n):
        out_ref[s] = jnp.concatenate(
            [result[b * steps_n + s : b * steps_n + s + 1] for b in range(batch)], axis=0
        ).astype(out_ref.dtype)

    @pl.loop(1, n)
    def _(i):
        remote(0, i, msg1.at[i], recv1.at[me], peer(i)).wait_send()
        remote(1, i, gath.at[me], gath.at[me], peer(i)).wait_send()
        remote(2, i, msg3.at[peer(i)], recv3.at[me], peer(i)).wait_send()
        remote(3, i, msg4.at[i], recv4.at[me], peer(i)).wait_send()


def local(
    hidden,
    norm_gain,
    w_query,
    w_key,
    w_value,
    w_output,
    key_cache,
    value_cache,
    retrieval,
    page_table,
    lengths,
    window_start,
):
    n = lax.axis_size("ctx")
    steps_n, batch, width_local = hidden.shape
    pages, page_len, kv_heads, dim = key_cache.shape
    query_width = w_query.shape[1]
    share = query_width // n
    rows = steps_n * batch
    q_rows = query_width // dim * steps_n
    if pages % 8 or (n, share, rows, batch, kv_heads, dim) != (2 * kv_heads, 4 * dim, 8, 2, 8, 128):
        return local_small(
            hidden,
            norm_gain,
            w_query,
            w_key,
            w_value,
            w_output,
            key_cache,
            value_cache,
            retrieval,
            page_table,
            lengths,
            window_start,
        )
    f32, bf16 = jnp.float32, jnp.bfloat16
    smem = pl.BlockSpec(memory_space=pltpu.SMEM)
    vmem = pl.BlockSpec(memory_space=pltpu.VMEM)
    hbm = pl.BlockSpec(memory_space=pl.ANY)
    dma = pltpu.SemaphoreType.DMA
    out = pl.pallas_call(
        functools.partial(fused, n, steps_n, batch, kv_heads, page_len),
        out_shape=jax.ShapeDtypeStruct((steps_n, batch, w_output.shape[1] // n), bf16),
        in_specs=[smem] * 3 + [vmem] * 3 + [hbm] * 6,
        out_specs=vmem,
        scratch_shapes=[
            pltpu.VMEM((n, width_local, share), bf16),
            pltpu.VMEM((width_local, 2 * kv_heads * dim), bf16),
            pltpu.VMEM((n, share, w_output.shape[1] // n), bf16),
            pltpu.VMEM((pages, page_len * kv_heads, dim), bf16),
            pltpu.VMEM((pages, page_len * kv_heads, dim), bf16),
            pltpu.VMEM((pages, dim, page_len * kv_heads), bf16),
            pltpu.VMEM((n, rows, share + 2 * dim), f32),
            pltpu.VMEM((n, rows, share + 2 * dim), f32),
            pltpu.VMEM((n, rows, share + dim), f32),
            pltpu.VMEM((batch, q_rows, dim), f32),
            pltpu.VMEM((batch, dim // (q_rows // kv_heads), dim, q_rows), bf16),
            pltpu.VMEM((4, pages, dim), jnp.int32),
            pltpu.SMEM((pages,), jnp.int32),
            pltpu.VMEM((pages, kv_heads, dim), f32),
            pltpu.VMEM((pages, kv_heads, dim), f32),
            pltpu.VMEM((pages, dim, q_rows), f32),
            pltpu.VMEM((n, 40, dim), f32),
            pltpu.VMEM((n, 40, dim), f32),
            pltpu.VMEM((n, rows, share), f32),
            pltpu.VMEM((n, rows, share), f32),
            dma((n,)),
            dma((n,)),
            dma((2,)),
            dma((pages,)),
            dma((pages,)),
            dma((4, n)),
            dma((4, n)),
        ],
        compiler_params=pltpu.CompilerParams(
            collective_id=0, has_side_effects=True, vmem_limit_bytes=56 * 2**20
        ),
    )(
        retrieval,
        lengths,
        window_start,
        hidden,
        norm_gain,
        page_table,
        w_query,
        w_key,
        w_value,
        w_output,
        key_cache.reshape(pages, page_len * kv_heads, dim),
        value_cache.reshape(pages, page_len * kv_heads, dim),
    )
    return out


def solution(mesh):
    placed = (
        P(None, "groups", "ctx"),
        P("ctx"),
        P("ctx", None),
        P("ctx", None),
        P("ctx", None),
        P("ctx", None),
        P(("groups", "ctx"), None, None, None),
        P(("groups", "ctx"), None, None, None),
        P(),
        P("groups", None),
        P("groups"),
        P("groups"),
    )
    return jax.shard_map(
        local, mesh=mesh, in_specs=placed, out_specs=P(None, "groups", "ctx"), check_vma=False
    )
```
